32 devices in a mesh: row: 2 (over x), col: 4 (over y, core), layer: 4 (over z).
Axes of the slice: x: 2, y: 2, z: 4, core: 2. Of those that a mesh axis runs over, the one named last changes fastest.
Arguments:
- source_matrix_strip: bfloat16 [4096, 512], P('row', 'col')
- target_matrix_strip: bfloat16 [512, 8192], P('row', ('col', 'layer'))
- stored_tile_flag: int32 [32, 4], P('row', 'col'), may hold values from 0 to 1
- target_place_tile_index: int32 [32, 32], P('row', ('col', 'layer')), may hold values from 0 to 3, as said below
- retained_target_flag: int32 [32, 32], P('row', ('col', 'layer')), may hold values 0 or 1
Outputs:
- clustered: bfloat16 [4096, 4096], P(('row', 'layer'), 'col')
The draws below stay inside these ranges and needn't reach their ends.
Inputs may be any that keep to these rules, and one draw needn't show every extreme that they name: `target_place_tile_index`: within each block row, the 2 slots of one column tile name distinct column blocks.
All inputs are finite; a program needn't handle non-finite values. No bound on the sum of `retained_target_flag` on one device may be relied on, other than what follows from the above.
Results may differ from the reference program's by a relative error of at most 0.0012.
Values may be sent and summed in bfloat16 or wider, within the bound.
No kernel may reach another device: no remote copies, remote signals or barrier semaphores. Data moves between devices by JAX's collectives and lax.ppermute only.
A program may use at most 64 MiB of HBM per device.

```python
import math
import jax
import jax.numpy as jnp
from jax import lax

BS = 128
COLB = 4
KOL = 2
BAND_COUNT_FULL = 32
ROWS_TOTAL = 4096
INNER = 512
COLS_TOTAL = 8192
TARGET_PLACES = 32
N_COL = 4
N_LAYER = 4


def draw_source_matrix_strip(key, part):
    key_base = jax.random.fold_in(key, 101)
    key_rows = jax.random.fold_in(key, 102)
    position = jnp.arange(ROWS_TOTAL, dtype=jnp.float32) / jnp.float32(max(ROWS_TOTAL - 1, 1))
    base = jnp.exp(jax.random.uniform(key_base, (ROWS_TOTAL, INNER), jnp.float32, math.log(0.05), 0.0))
    spread = jnp.exp(jax.random.uniform(key_rows, (ROWS_TOTAL,), jnp.float32, 0.0, math.log(4.0)))
    scales = jnp.exp(position * math.log(3.0)) * spread
    return (base * scales[:, None]).astype(jnp.bfloat16)


def draw_target_matrix_strip(key, part):
    key_base = jax.random.fold_in(key, 201)
    key_cols = jax.random.fold_in(key, 202)
    base = jnp.exp(jax.random.uniform(key_base, (INNER, COLS_TOTAL), jnp.float32, math.log(0.05), 0.0))
    scales = jnp.exp(jax.random.uniform(key_cols, (COLS_TOTAL,), jnp.float32, 0.0, math.log(10.0)))
    return (base * scales[None, :]).astype(jnp.bfloat16)


def draw_stored_tile_flag(key, part):
    key_level = jax.random.fold_in(key, 301)
    key_value = jax.random.fold_in(key, 302)
    level = jax.random.randint(key_level, (BAND_COUNT_FULL, 1), 1, 6)
    values = jax.random.randint(key_value, (BAND_COUNT_FULL, N_COL), 0, 5)
    return (values < level).astype(jnp.int32)


def draw_target_place_tile_index(key, part):
    key_first = jax.random.fold_in(key, 401)
    key_step = jax.random.fold_in(key, 402)
    tiles = N_COL * N_LAYER
    first = jax.random.randint(key_first, (BAND_COUNT_FULL, tiles), 0, COLB)
    step = jax.random.randint(key_step, (BAND_COUNT_FULL, tiles), 1, COLB)
    second = (first + step) % COLB
    return jnp.stack([first, second], axis=2).reshape(BAND_COUNT_FULL, TARGET_PLACES).astype(jnp.int32)


def plant(values, own_key, low, largest):
    longest = values.shape.index(max(values.shape))
    spots = []
    for shift in (0, 1):
        where = [jax.random.randint(jax.random.fold_in(own_key, axis), (), 0, length) for axis, length in enumerate(values.shape)]
        where[longest] = (where[longest] + shift) % values.shape[longest]
        spots.append(tuple(where))
    return values.at[spots[0]].set(low).at[spots[1]].set(largest)


def setup_inputs(seed: int = 0) -> dict:
    streams_of = jax.random.split(jax.random.key(seed), 6)
    source_matrix_strip = draw_source_matrix_strip(jax.random.fold_in(streams_of[5], 71), 0)
    target_matrix_strip = draw_target_matrix_strip(jax.random.fold_in(streams_of[5], 71), 0)
    stored_tile_flag = draw_stored_tile_flag(jax.random.fold_in(streams_of[5], 71), 0)
    target_place_tile_index = draw_target_place_tile_index(jax.random.fold_in(streams_of[5], 71), 0)
    retained_target_flag = plant((jax.random.randint(streams_of[4], (BAND_COUNT_FULL, TARGET_PLACES), 0, 4) < 3).astype(jnp.int32), jax.random.fold_in(streams_of[4], 1), 0, 1)
    return {"source_matrix_strip": source_matrix_strip, "target_matrix_strip": target_matrix_strip, "stored_tile_flag": stored_tile_flag, "target_place_tile_index": target_place_tile_index, "retained_target_flag": retained_target_flag}


def reference(source_matrix_strip, target_matrix_strip, stored_tile_flag, target_place_tile_index, retained_target_flag):
    expanded = jnp.repeat(jnp.repeat(stored_tile_flag, BS, axis=0), BS, axis=1)
    masked = source_matrix_strip * expanded.astype(jnp.bfloat16)
    tiles = N_COL * N_LAYER
    right_tiles = target_matrix_strip.reshape(INNER, tiles, COLB, BS)
    tile_ids = (jnp.arange(TARGET_PLACES, dtype=jnp.int32) // KOL).astype(jnp.int32)

    def one_row(operands):
        block_rows, slot_ids = operands
        chosen = right_tiles[:, tile_ids, slot_ids.astype(jnp.int32), :]
        chosen = chosen.reshape(INNER, TARGET_PLACES * BS)
        return jnp.dot(block_rows, chosen, preferred_element_type=jnp.float32)

    picked = lax.map(one_row, (masked.reshape(BAND_COUNT_FULL, BS, INNER), target_place_tile_index))
    picked = picked.reshape(BAND_COUNT_FULL, BS, TARGET_PLACES, BS)
    retain_weight = retained_target_flag.astype(jnp.float32)
    raised_power_blocks = picked * picked * retain_weight[:, None, :, None]
    global_ids = (tile_ids[None, :] * COLB + target_place_tile_index).astype(jnp.int32)
    row_sums = jnp.sum(raised_power_blocks, axis=1)
    column_sums = jax.ops.segment_sum(row_sums.reshape(-1, BS), global_ids.reshape(-1), num_segments=tiles * COLB)
    column_mean = column_sums / jnp.float32(ROWS_TOTAL)
    denominator = column_mean[global_ids] + 1e-6
    clustered = raised_power_blocks / denominator[:, None, :, :]
    return clustered.astype(jnp.bfloat16).reshape(ROWS_TOTAL, TARGET_PLACES * BS)
```

```python
import functools

import jax
import jax.numpy as jnp
from jax import lax
from jax.experimental import pallas as pl
from jax.experimental.pallas import tpu as pltpu
from jax.sharding import PartitionSpec as P

BS = 128
COLB = 4
KOL = 2
TILE = COLB * BS
OUT = KOL * BS
META = COLB
VMEM_LIMIT = 48 * 1024 * 1024

ANY = pl.BlockSpec(memory_space=pl.ANY)
VMEM = pl.BlockSpec(memory_space=pltpu.VMEM)
SMEM = pl.BlockSpec(memory_space=pltpu.SMEM)


def swap(value, axis, bit):
    count = lax.axis_size(axis)
    return lax.ppermute(value, axis, [(i, i ^ bit) for i in range(count)])


def gather(piece, axis):
    count = lax.axis_size(axis)
    pieces = {0: piece}
    bit = count // 2
    while bit:
        for k in list(pieces):
            pieces[k ^ bit] = swap(pieces[k], axis, bit)
        bit //= 2
    return [pieces[k] for k in range(count)]


def call(kernel, out_shape, in_specs, out_specs, scratch, flops, nbytes, aliases=None):
    return pl.pallas_call(
        kernel,
        out_shape=out_shape,
        in_specs=in_specs,
        out_specs=out_specs,
        scratch_shapes=scratch,
        input_output_aliases=aliases or {},
        compiler_params=pltpu.CompilerParams(vmem_limit_bytes=VMEM_LIMIT),
        cost_estimate=pl.CostEstimate(flops=flops, bytes_accessed=nbytes, transcendentals=0),
    )


def mask_kernel(flag, source, masked):
    for i in range(source.shape[0] // BS):
        rows = pl.ds(i * BS, BS)
        block = source[rows, :]
        masked[rows, :] = jnp.where(flag[0, i] != 0, block, jnp.zeros_like(block))


def mask_blocks(flag, source):
    size = source.size * 2
    return call(
        mask_kernel,
        jax.ShapeDtypeStruct(source.shape, source.dtype),
        [SMEM, VMEM],
        VMEM,
        [],
        source.size,
        2 * size,
    )(flag, source)


def fetch_left(lefts, panel, sem):
    me = lax.axis_index("col")
    copies = []
    for k, left in enumerate(lefts):
        place = pl.ds(pl.multiple_of((me ^ k) * BS, BS), BS)
        copies.append(pltpu.make_async_copy(left, panel.at[:, place], sem.at[k]))
    return copies


def fetch_right(rights, panel, sem):
    me = lax.axis_index("row")
    depth = rights[0].shape[0]
    copies = []
    for k, right in enumerate(rights):
        place = pl.ds(pl.multiple_of((me ^ k) * depth, depth), depth)
        copies.append(pltpu.make_async_copy(right, panel.at[place, :], sem.at[k]))
    return copies


def own_tile_kernel(n_left, n_right, layers, *refs):
    place_s, keep_s, place_v, keep_v = refs[:4]
    lefts = refs[4 : 4 + n_left]
    rights = refs[4 + n_left : 4 + n_left + n_right]
    sums, inflated, own_left = refs[4 + n_left + n_right : 7 + n_left + n_right]
    left, right, product, kept, partial, left_sem, right_sem, out_sem = refs[7 + n_left + n_right :]
    layer = lax.axis_index("layer")
    copies = fetch_left(lefts, left, left_sem) + fetch_right(rights, right, right_sem)
    for copy in copies:
        copy.start()
    partial[...] = jnp.zeros_like(partial)
    for copy in copies:
        copy.wait()
    band = left.shape[0] // layers
    own_rows = pl.ds(pl.multiple_of(layer * band, band), band)
    left_out = pltpu.make_async_copy(left.at[own_rows, :], own_left, out_sem.at[0])
    left_out.start()

    @pl.loop(0, layers)
    def _(q):
        first = pl.multiple_of(q * band, band)
        product[...] = jnp.dot(
            left[pl.ds(first, band), :], right[...], preferred_element_type=jnp.float32
        )
        for i in range(band // BS):
            for s in range(KOL):
                row = q * (band // BS) + i
                block = place_s[s, row]
                picked = product[
                    pl.ds(i * BS, BS), pl.ds(pl.multiple_of(block * BS, BS), BS)
                ]
                squares = picked * picked * keep_s[s, row].astype(jnp.float32)
                kept[pl.ds(pl.multiple_of(first + i * BS, BS), BS), pl.ds(s * BS, BS)] = squares
                partial[block] += jnp.sum(squares.reshape(BS // 8, 8, BS), axis=0)

    for part in range(2):
        rows = pl.ds(pl.multiple_of((layer ^ part) * band, band), band)
        pltpu.make_async_copy(kept.at[rows, :], inflated.at[pl.ds(part * band, band), :], out_sem.at[1 + part]).start()
    sums[...] = jnp.zeros_like(sums)
    for block in range(COLB):
        sums[pl.ds(block, 1), :] = jnp.sum(partial[block], axis=0, keepdims=True)
    bands = place_v.shape[1]
    sums[META : META + KOL, 0:bands] = place_v[...].astype(jnp.float32)
    sums[META + KOL : META + 2 * KOL, 0:bands] = keep_v[...].astype(jnp.float32)
    left_out.wait()
    for part in range(2):
        rows = pl.ds(pl.multiple_of((layer ^ part) * band, band), band)
        pltpu.make_async_copy(kept.at[rows, :], inflated.at[pl.ds(part * band, band), :], out_sem.at[1 + part]).wait()


def own_tile(place, keep, lefts, rights, layers):
    rows = lefts[0].shape[0]
    inner = len(lefts) * BS
    band = rows // layers
    return call(
        functools.partial(own_tile_kernel, len(lefts), len(rights), layers),
        (
            jax.ShapeDtypeStruct((2 * COLB, BS), jnp.float32),
            jax.ShapeDtypeStruct((2 * band, OUT), jnp.float32),
            jax.ShapeDtypeStruct((band, inner), jnp.bfloat16),
        ),
        [SMEM, SMEM, VMEM, VMEM] + [ANY] * (len(lefts) + len(rights)),
        (VMEM, ANY, ANY),
        [
            pltpu.VMEM((rows, inner), jnp.bfloat16),
            pltpu.VMEM((inner, TILE), jnp.bfloat16),
            pltpu.VMEM((band, TILE), jnp.float32),
            pltpu.VMEM((rows, OUT), jnp.float32),
            pltpu.VMEM((COLB, 8, BS), jnp.float32),
            pltpu.SemaphoreType.DMA((len(lefts),)),
            pltpu.SemaphoreType.DMA((len(rights),)),
            pltpu.SemaphoreType.DMA((3,)),
        ],
        2 * rows * inner * TILE,
        2 * (rows + TILE) * inner + 4 * rows * OUT,
    )(place, keep, place, keep, *lefts, *rights)


def scale_kernel(total_rows, place, sums, other, inflated, out, sent, all_sums, own, scale, sem):
    layer = lax.axis_index("layer")
    whole = sums[0:COLB, :] + other[0:COLB, :]
    all_sums[...] = sums[...]
    all_sums[0:COLB, :] = whole
    scale[...] = 1.0 / (whole / jnp.float32(total_rows) + 1e-6)
    band = own.shape[0]
    for part, target in ((1, sent), (0, own)):
        for i in range(band // BS):
            row = (layer ^ part) * (band // BS) + i
            for s in range(KOL):
                at = (pl.ds(part * band + i * BS, BS), pl.ds(s * BS, BS))
                to = (pl.ds(i * BS, BS), pl.ds(s * BS, BS))
                block = place[s, row]
                target[to] = (inflated[at] * scale[pl.ds(block, 1), :]).astype(target.dtype)
    columns = pl.ds(pl.multiple_of(layer * OUT, OUT), OUT)
    copy = pltpu.make_async_copy(own, out.at[:, columns], sem)
    copy.start()
    copy.wait()


def scale_own(place, sums, other, inflated, layers, total_rows):
    band = inflated.shape[0] // 2
    return call(
        functools.partial(scale_kernel, total_rows),
        (
            jax.ShapeDtypeStruct((band, layers * OUT), jnp.bfloat16),
            jax.ShapeDtypeStruct((band, OUT), jnp.bfloat16),
            jax.ShapeDtypeStruct(sums.shape, jnp.float32),
        ),
        [SMEM, VMEM, VMEM, VMEM],
        (ANY, VMEM, VMEM),
        [
            pltpu.VMEM((band, OUT), jnp.bfloat16),
            pltpu.VMEM((COLB, BS), jnp.float32),
            pltpu.SemaphoreType.DMA,
        ],
        4 * inflated.size,
        6 * inflated.size,
    )(place, sums, other, inflated)


def far_tile_kernel(n_right, bit, total_rows, with_sent, *refs):
    sums_s, sums, own_left = refs[:3]
    rights = refs[3 : 3 + n_right]
    rest = refs[3 + n_right :]
    sent = None
    if with_sent:
        sent, rest = rest[0], rest[1:]
    _, out, right, product, result, scale, right_sem, out_sem = rest
    layer = lax.axis_index("layer")
    copies = fetch_right(rights, right, right_sem)
    for copy in copies:
        copy.start()
    outs = []
    if with_sent:
        columns = pl.ds(pl.multiple_of((layer ^ 1) * OUT, OUT), OUT)
        outs.append(pltpu.make_async_copy(sent, out.at[:, columns], out_sem.at[1]))
        outs[0].start()
    scale[...] = 1.0 / (sums[0:COLB, :] / jnp.float32(total_rows) + 1e-6)
    for copy in copies:
        copy.wait()
    product[...] = jnp.dot(own_left[...], right[...], preferred_element_type=jnp.float32)
    bands = own_left.shape[0] // BS
    for i in range(bands):
        for s in range(KOL):
            row = layer * bands + i
            block = sums_s[META + s, row].astype(jnp.int32)
            keep = sums_s[META + KOL + s, row]
            picked = product[pl.ds(i * BS, BS), pl.ds(pl.multiple_of(block * BS, BS), BS)]
            squares = picked * picked * keep
            result[pl.ds(i * BS, BS), pl.ds(s * BS, BS)] = (
                squares * scale[pl.ds(block, 1), :]
            ).astype(result.dtype)
    columns = pl.ds(pl.multiple_of((layer ^ bit) * OUT, OUT), OUT)
    outs.append(pltpu.make_async_copy(result, out.at[:, columns], out_sem.at[0]))
    outs[-1].start()
    for copy in outs:
        copy.wait()


def far_tile(sums, own_left, rights, sent, out, bit, total_rows):
    band, inner = own_left.shape
    extra = [] if sent is None else [sent]
    operands = [sums, sums, own_left, *rights, *extra, out]
    return call(
        functools.partial(far_tile_kernel, len(rights), bit, total_rows, sent is not None),
        jax.ShapeDtypeStruct(out.shape, out.dtype),
        [SMEM, VMEM, VMEM] + [ANY] * (len(rights) + len(extra) + 1),
        ANY,
        [
            pltpu.VMEM((inner, TILE), jnp.bfloat16),
            pltpu.VMEM((band, TILE), jnp.float32),
            pltpu.VMEM((band, OUT), jnp.bfloat16),
            pltpu.VMEM((COLB, BS), jnp.float32),
            pltpu.SemaphoreType.DMA((len(rights),)),
            pltpu.SemaphoreType.DMA((2,)),
        ],
        2 * band * inner * TILE,
        2 * (band + TILE) * inner + 2 * band * OUT,
        {len(operands) - 1: 0},
    )(*operands)


def shards(
    source_matrix_strip,
    target_matrix_strip,
    stored_tile_flag,
    target_place_tile_index,
    retained_target_flag,
):
    layers = lax.axis_size("layer")
    total_rows = source_matrix_strip.shape[0] * lax.axis_size("row")
    place = target_place_tile_index.T
    keep = retained_target_flag.T
    masked = mask_blocks(stored_tile_flag.T, source_matrix_strip)
    lefts = gather(masked, "col")
    near = gather(target_matrix_strip, "row")
    far = swap(target_matrix_strip, "layer", 2)
    sums, inflated, own_left = own_tile(place, keep, lefts, near, layers)
    opposite = swap(far, "layer", 1)
    far_pieces = gather(far, "row")
    opposite_pieces = gather(opposite, "row")
    bit = lax.axis_size("row") // 2
    while bit > 1:
        other = swap(sums, "row", bit)
        sums = jnp.concatenate([sums[:COLB] + other[:COLB], sums[COLB:]])
        bit //= 2
    other = swap(sums, "row", 1)
    out, sent, sums = scale_own(place, sums, other, inflated, layers, total_rows)
    sent = swap(sent, "layer", 1)
    far_sums = swap(sums, "layer", 2)
    opposite_sums = swap(far_sums, "layer", 1)
    out = far_tile(far_sums, own_left, far_pieces, None, out, 2, total_rows)
    return far_tile(opposite_sums, own_left, opposite_pieces, sent, out, 3, total_rows)


def solution(mesh):
    placed = (
        P("row", "col"),
        P("row", ("col", "layer")),
        P("row", "col"),
        P("row", ("col", "layer")),
        P("row", ("col", "layer")),
    )
    return jax.shard_map(
        shards, mesh=mesh, in_specs=placed, out_specs=P(("row", "layer"), "col"), check_vma=False
    )
```

```python
import functools

import jax
import jax.numpy as jnp
from jax import lax
from jax.experimental import pallas as pl
from jax.experimental.pallas import tpu as pltpu
from jax.sharding import PartitionSpec as P

BS = 128
COLB = 4
KOL = 2
TILE = COLB * BS
OUT = KOL * BS
META = COLB
VMEM_LIMIT = 48 * 1024 * 1024

ANY = pl.BlockSpec(memory_space=pl.ANY)
VMEM = pl.BlockSpec(memory_space=pltpu.VMEM)
SMEM = pl.BlockSpec(memory_space=pltpu.SMEM)


def swap(value, axis, bit):
    count = lax.axis_size(axis)
    return lax.ppermute(value, axis, [(i, i ^ bit) for i in range(count)])


def spread(piece, axis, count):
    pieces = {0: piece}
    bit = count // 2
    while bit:
        for k in list(pieces):
            pieces[k ^ bit] = swap(pieces[k], axis, bit)
        bit //= 2
    return [pieces[k] for k in range(count)]


def gather(piece, axis):
    return spread(piece, axis, lax.axis_size(axis))


def call(kernel, out_shape, in_specs, out_specs, scratch, flops, nbytes, aliases=None):
    return pl.pallas_call(
        kernel,
        out_shape=out_shape,
        in_specs=in_specs,
        out_specs=out_specs,
        scratch_shapes=scratch,
        input_output_aliases=aliases or {},
        compiler_params=pltpu.CompilerParams(vmem_limit_bytes=VMEM_LIMIT),
        cost_estimate=pl.CostEstimate(flops=flops, bytes_accessed=nbytes, transcendentals=0),
    )


def mask_kernel(flag, source, masked):
    for i in range(source.shape[0] // BS):
        rows = pl.ds(i * BS, BS)
        block = source[rows, :]
        masked[rows, :] = jnp.where(flag[0, i] != 0, block, jnp.zeros_like(block))


def mask_blocks(flag, source):
    size = source.size * 2
    return call(
        mask_kernel,
        jax.ShapeDtypeStruct(source.shape, source.dtype),
        [SMEM, VMEM],
        VMEM,
        [],
        source.size,
        2 * size,
    )(flag, source)


def fetch_right(rights, panel, sem):
    me = lax.axis_index("row")
    depth = rights[0].shape[0]
    copies = []
    for k, right in enumerate(rights):
        place = pl.ds(pl.multiple_of((me ^ k) * depth, depth), depth)
        copies.append(pltpu.make_async_copy(right, panel.at[place, :], sem.at[k]))
    return copies


def partial_product(lefts, first_k, right, rows):
    me = lax.axis_index("col")
    deep = jnp.concatenate([left[rows, :] for left in lefts], axis=1)
    blocks = []
    for k in range(len(lefts)):
        place = pl.ds(pl.multiple_of((me ^ (first_k + k)) * BS, BS), BS)
        blocks.append(right[place, :])
    return jnp.dot(deep, jnp.concatenate(blocks, axis=0), preferred_element_type=jnp.float32)


def early_kernel(n_left, n_right, band, *refs):
    place = refs[0]
    lefts = refs[1 : 1 + n_left]
    rights = refs[1 + n_left : 1 + n_left + n_right]
    right, picked, product, sem = refs[1 + n_left + n_right :]
    copies = fetch_right(rights, right, sem)
    for copy in copies:
        copy.start()
    for copy in copies:
        copy.wait()

    @pl.loop(0, picked.shape[0] // band)
    def _(q):
        first = pl.multiple_of(q * band, band)
        product[...] = partial_product(lefts, 0, right, pl.ds(first, band))
        for i in range(band // BS):
            rows = pl.ds(pl.multiple_of(first + i * BS, BS), BS)
            for s in range(KOL):
                block = place[s, q * (band // BS) + i]
                picked[rows, pl.ds(s * BS, BS)] = product[
                    pl.ds(i * BS, BS), pl.ds(pl.multiple_of(block * BS, BS), BS)
                ]


def early(place, lefts, rights, band):
    rows = lefts[0].shape[0]
    inner = sum(right.shape[0] for right in rights)
    return call(
        functools.partial(early_kernel, len(lefts), len(rights), band),
        (
            jax.ShapeDtypeStruct((inner, TILE), jnp.bfloat16),
            jax.ShapeDtypeStruct((rows, OUT), jnp.float32),
        ),
        [SMEM] + [VMEM] * len(lefts) + [ANY] * len(rights),
        (VMEM, VMEM),
        [pltpu.VMEM((band, TILE), jnp.float32), pltpu.SemaphoreType.DMA((len(rights),))],
        rows * inner * TILE,
        2 * (rows // 2 + TILE) * inner + 4 * rows * OUT,
    )(place, *lefts, *rights)


def late_kernel(n_left, band, place, keep, place_v, keep_v, right, picked, *refs):
    lefts = refs[:n_left]
    sums, meta, inflated, own_left, product, partial = refs[n_left:]
    lates = lefts[n_left // 2 :]
    layer = lax.axis_index("layer")
    me = lax.axis_index("col")
    partial[...] = jnp.zeros_like(partial)

    @pl.loop(0, picked.shape[0] // band)
    def _(q):
        first = pl.multiple_of(q * band, band)
        product[...] = partial_product(lates, n_left // 2, right, pl.ds(first, band))
        for i in range(band // BS):
            rows = pl.ds(pl.multiple_of(first + i * BS, BS), BS)
            for s in range(KOL):
                row = q * (band // BS) + i
                block = place[s, row]
                late = product[pl.ds(i * BS, BS), pl.ds(pl.multiple_of(block * BS, BS), BS)]
                whole = picked[rows, pl.ds(s * BS, BS)] + late
                squares = whole * whole * keep[s, row].astype(jnp.float32)
                partial[block] += jnp.sum(squares.reshape(BS // 8, 8, BS), axis=0)
                for part in range(2):

                    @pl.when(q == layer ^ part)
                    def _():
                        inflated[pl.ds(part * band + i * BS, BS), pl.ds(s * BS, BS)] = squares

    for block in range(COLB):
        sums[pl.ds(block, 1), :] = jnp.sum(partial[block], axis=0, keepdims=True)
    bands = place_v.shape[1]
    meta[...] = jnp.zeros_like(meta)
    meta[0:KOL, 0:bands] = place_v[...].astype(jnp.float32)
    meta[KOL : 2 * KOL, 0:bands] = keep_v[...].astype(jnp.float32)
    own_rows = pl.ds(pl.multiple_of(layer * band, band), band)
    for k, left in enumerate(lefts):
        place_k = pl.ds(pl.multiple_of((me ^ k) * BS, BS), BS)
        own_left[:, place_k] = left[own_rows, :]


def late(place, keep, right, picked, lefts, band):
    rows = picked.shape[0]
    inner = right.shape[0]
    return call(
        functools.partial(late_kernel, len(lefts), band),
        (
            jax.ShapeDtypeStruct((COLB, BS), jnp.float32),
            jax.ShapeDtypeStruct((2 * KOL, BS), jnp.float32),
            jax.ShapeDtypeStruct((2 * band, OUT), jnp.float32),
            jax.ShapeDtypeStruct((band, inner), jnp.bfloat16),
        ),
        [SMEM, SMEM] + [VMEM] * (4 + len(lefts)),
        (VMEM, VMEM, VMEM, VMEM),
        [pltpu.VMEM((band, TILE), jnp.float32), pltpu.VMEM((COLB, 8, BS), jnp.float32)],
        rows * inner * TILE,
        2 * (rows // 2 + TILE) * inner + 4 * rows * OUT,
    )(place, keep, place, keep, right, picked, *lefts)


def scaled(place_of, inflated, first, scale, target):
    for i in range(target.shape[0] // BS):
        for s in range(KOL):
            at = (pl.ds(first + i * BS, BS), pl.ds(s * BS, BS))
            to = (pl.ds(i * BS, BS), pl.ds(s * BS, BS))
            row = scale[pl.ds(place_of(s, i), 1), :]
            target[to] = (inflated[at] * row).astype(target.dtype)


def scale_kernel(total_rows, place, sums, other, meta, inflated, sent, all_sums, scale):
    layer = lax.axis_index("layer")
    whole = sums[...] + other[...]
    all_sums[0:COLB, :] = whole
    all_sums[META : META + 2 * KOL, :] = meta[...]
    scale[...] = 1.0 / (whole / jnp.float32(total_rows) + 1e-6)
    band = sent.shape[0]
    bands = band // BS
    scaled(lambda s, i: place[s, (layer ^ 1) * bands + i], inflated, band, scale, sent)


def scale_sent(place, sums, other, meta, inflated, total_rows):
    band = inflated.shape[0] // 2
    return call(
        functools.partial(scale_kernel, total_rows),
        (
            jax.ShapeDtypeStruct((band, OUT), jnp.bfloat16),
            jax.ShapeDtypeStruct((COLB + 2 * KOL, BS), jnp.float32),
        ),
        [SMEM, VMEM, VMEM, VMEM, VMEM],
        (VMEM, VMEM),
        [pltpu.VMEM((COLB, BS), jnp.float32)],
        2 * inflated.size,
        3 * inflated.size,
    )(place, sums, other, meta, inflated)


def far_result(sums_s, sums, own_left, rights, total_rows, product, scale, result):
    layer = lax.axis_index("layer")
    me = lax.axis_index("row")
    scale[...] = 1.0 / (sums[0:COLB, :] / jnp.float32(total_rows) + 1e-6)
    depth = rights[0].shape[0]
    whole = None
    for k, right in enumerate(rights):
        place = pl.ds(pl.multiple_of((me ^ k) * depth, depth), depth)
        term = jnp.dot(own_left[:, place], right[...], preferred_element_type=jnp.float32)
        whole = term if whole is None else whole + term
    product[...] = whole
    bands = own_left.shape[0] // BS
    for i in range(bands):
        for s in range(KOL):
            row = layer * bands + i
            block = sums_s[META + s, row].astype(jnp.int32)
            keep = sums_s[META + KOL + s, row]
            picked = product[pl.ds(i * BS, BS), pl.ds(pl.multiple_of(block * BS, BS), BS)]
            squares = picked * picked * keep
            result[pl.ds(i * BS, BS), pl.ds(s * BS, BS)] = (
                squares * scale[pl.ds(block, 1), :]
            ).astype(result.dtype)


def columns_of(layer):
    return pl.ds(pl.multiple_of(layer * OUT, OUT), OUT)


def first_tiles_kernel(n_right, total_rows, place, sums_s, sums, own_left, own_sums, inflated, *refs):
    rights = refs[:n_right]
    out, product, scale, own, result, sem = refs[n_right:]
    layer = lax.axis_index("layer")
    scale[...] = 1.0 / (own_sums[0:COLB, :] / jnp.float32(total_rows) + 1e-6)
    bands = own.shape[0] // BS
    scaled(lambda s, i: place[s, layer * bands + i], inflated, 0, scale, own)
    own_copy = pltpu.make_async_copy(own, out.at[:, columns_of(layer)], sem.at[0])
    own_copy.start()
    far_result(sums_s, sums, own_left, rights, total_rows, product, scale, result)
    far_copy = pltpu.make_async_copy(result, out.at[:, columns_of(layer ^ 2)], sem.at[1])
    far_copy.start()
    own_copy.wait()
    far_copy.wait()


def first_tiles(place, sums, own_left, own_sums, inflated, rights, layers, total_rows):
    band, inner = own_left.shape
    return call(
        functools.partial(first_tiles_kernel, len(rights), total_rows),
        jax.ShapeDtypeStruct((band, layers * OUT), jnp.bfloat16),
        [SMEM, SMEM] + [VMEM] * (4 + len(rights)),
        ANY,
        [
            pltpu.VMEM((band, TILE), jnp.float32),
            pltpu.VMEM((COLB, BS), jnp.float32),
            pltpu.VMEM((band, OUT), jnp.bfloat16),
            pltpu.VMEM((band, OUT), jnp.bfloat16),
            pltpu.SemaphoreType.DMA((2,)),
        ],
        2 * band * inner * TILE,
        2 * (band + TILE) * inner + 2 * band * OUT,
    )(place, sums, sums, own_left, own_sums, inflated, *rights)


def last_tiles_kernel(n_right, total_rows, sums_s, sums, own_left, sent, *refs):
    rights = refs[:n_right]
    _, out, product, scale, result, sem = refs[n_right:]
    layer = lax.axis_index("layer")
    sent_copy = pltpu.make_async_copy(sent, out.at[:, columns_of(layer ^ 1)], sem.at[0])
    sent_copy.start()
    far_result(sums_s, sums, own_left, rights, total_rows, product, scale, result)
    far_copy = pltpu.make_async_copy(result, out.at[:, columns_of(layer ^ 3)], sem.at[1])
    far_copy.start()
    sent_copy.wait()
    far_copy.wait()


def last_tiles(sums, own_left, sent, rights, out, total_rows):
    band, inner = own_left.shape
    return call(
        functools.partial(last_tiles_kernel, len(rights), total_rows),
        jax.ShapeDtypeStruct(out.shape, out.dtype),
        [SMEM] + [VMEM] * (3 + len(rights)) + [ANY],
        ANY,
        [
            pltpu.VMEM((band, TILE), jnp.float32),
            pltpu.VMEM((COLB, BS), jnp.float32),
            pltpu.VMEM((band, OUT), jnp.bfloat16),
            pltpu.SemaphoreType.DMA((2,)),
        ],
        2 * band * inner * TILE,
        2 * (band + TILE) * inner + 2 * band * OUT,
        {4 + len(rights): 0},
    )(sums, sums, own_left, sent, *rights, out)


def shards(
    source_matrix_strip,
    target_matrix_strip,
    stored_tile_flag,
    target_place_tile_index,
    retained_target_flag,
):
    layers = lax.axis_size("layer")
    total_rows = source_matrix_strip.shape[0] * lax.axis_size("row")
    band = source_matrix_strip.shape[0] // layers
    place = target_place_tile_index.T
    keep = retained_target_flag.T
    half = lax.axis_size("col") // 2
    far = swap(target_matrix_strip, "layer", 2)
    masked = mask_blocks(stored_tile_flag.T, source_matrix_strip)
    across = swap(masked, "col", half)
    near = gather(target_matrix_strip, "row")
    earlies = spread(masked, "col", half)
    right, picked = early(place, earlies, near, band)
    across, far, picked = lax.optimization_barrier((across, far, picked))
    opposite = swap(far, "layer", 1)
    lates = spread(across, "col", half)
    far_pieces = gather(far, "row")
    sums, meta, inflated, own_left = late(place, keep, right, picked, earlies + lates, band)
    opposite_pieces = gather(opposite, "row")
    bit = lax.axis_size("row") // 2
    while bit > 1:
        sums = sums + swap(sums, "row", bit)
        bit //= 2
    other = swap(sums, "row", 1)
    sent, sums = scale_sent(place, sums, other, meta, inflated, total_rows)
    sent = swap(sent, "layer", 1)
    far_sums = swap(sums, "layer", 2)
    opposite_sums = swap(sums, "layer", 3)
    out = first_tiles(place, far_sums, own_left, sums, inflated, far_pieces, layers, total_rows)
    return last_tiles(opposite_sums, own_left, sent, opposite_pieces, out, total_rows)


def solution(mesh):
    placed = (
        P("row", "col"),
        P("row", ("col", "layer")),
        P("row", "col"),
        P("row", ("col", "layer")),
        P("row", ("col", "layer")),
    )
    return jax.shard_map(
        shards, mesh=mesh, in_specs=placed, out_specs=P(("row", "layer"), "col"), check_vma=False
    )
```

```python
import functools

import jax
import jax.numpy as jnp
from jax import lax
from jax.experimental import pallas as pl
from jax.experimental.pallas import tpu as pltpu
from jax.sharding import PartitionSpec as P

BS = 128
COLB = 4
KOL = 2
TILE = COLB * BS
OUT = KOL * BS
CHUNKS = 2
VMEM_LIMIT = 12 * 1024 * 1024

HBM = pl.BlockSpec(memory_space=pltpu.HBM)
VMEM = pl.BlockSpec(memory_space=pltpu.VMEM)


def swap(value, axis, bit):
    count = lax.axis_size(axis)
    return lax.ppermute(value, axis, [(i, i ^ bit) for i in range(count)])


def spread(piece, axis, count):
    pieces = {0: piece}
    bit = count // 2
    while bit:
        for k in list(pieces):
            pieces[k ^ bit] = swap(pieces[k], axis, bit)
        bit //= 2
    return [pieces[k] for k in range(count)]


def gather(piece, axis):
    return spread(piece, axis, lax.axis_size(axis))


def in_hbm(*values):
    return [pltpu.with_memory_space_constraint(value, pltpu.HBM) for value in values]


def call(kernel, out_shape, in_specs, out_specs, scratch, flops, nbytes, aliases=None):
    return pl.pallas_call(
        kernel,
        out_shape=out_shape,
        in_specs=in_specs,
        out_specs=out_specs,
        scratch_shapes=scratch,
        input_output_aliases=aliases or {},
        compiler_params=pltpu.CompilerParams(vmem_limit_bytes=VMEM_LIMIT),
        cost_estimate=pl.CostEstimate(flops=flops, bytes_accessed=nbytes, transcendentals=0),
    )


def mask_kernel(flag, source, place, keep, *refs):
    masked = refs[:CHUNKS]
    meta, flag_s, panel, meta_v, sem, flag_sem, meta_sem = refs[CHUNKS:]
    rows = source.shape[0] // CHUNKS
    flag_copy = pltpu.make_async_copy(flag, flag_s, flag_sem)
    flag_copy.start()
    copies = []
    for c in range(CHUNKS):
        part = pl.ds(c * rows, rows)
        copies.append(pltpu.make_async_copy(source.at[part, :], panel.at[part, :], sem.at[c]))
        copies[c].start()
    metas = [
        pltpu.make_async_copy(place, meta_v.at[0:KOL, :], meta_sem.at[0]),
        pltpu.make_async_copy(keep, meta_v.at[KOL : 2 * KOL, :], meta_sem.at[1]),
    ]
    for copy in metas:
        copy.start()
    flag_copy.wait()
    for c in range(CHUNKS):
        copies[c].wait()
        for i in range(rows // BS):
            block = panel[pl.ds(c * rows + i * BS, BS), :]
            kept = flag_s[0, c * (rows // BS) + i] != 0
            masked[c][pl.ds(i * BS, BS), :] = jnp.where(kept, block, jnp.zeros_like(block))
    for copy in metas:
        copy.wait()
    meta[...] = jnp.zeros_like(meta)
    meta[:, 0 : meta_v.shape[1]] = meta_v[...].astype(jnp.float32)


def mask_blocks(flag, source, place, keep):
    rows = source.shape[0]
    *masked, meta = call(
        mask_kernel,
        [jax.ShapeDtypeStruct((rows // CHUNKS, BS), source.dtype)] * CHUNKS
        + [jax.ShapeDtypeStruct((2 * KOL, BS), jnp.float32)],
        [HBM, HBM, HBM, HBM],
        [VMEM] * (CHUNKS + 1),
        [
            pltpu.SMEM(flag.shape, jnp.int32),
            pltpu.VMEM(source.shape, source.dtype),
            pltpu.VMEM((2 * KOL, place.shape[1]), jnp.int32),
            pltpu.SemaphoreType.DMA((CHUNKS,)),
            pltpu.SemaphoreType.DMA,
            pltpu.SemaphoreType.DMA((2,)),
        ],
        source.size,
        4 * source.size,
    )(*in_hbm(flag, source, place, keep))
    return masked, meta


def product_of(lefts, right, rows):
    me = lax.axis_index("col")
    deep = jnp.concatenate([left[rows, :] for left in lefts], axis=1)
    blocks = []
    for k in range(len(lefts)):
        place = pl.ds(pl.multiple_of((me ^ k) * BS, BS), BS)
        blocks.append(right[place, :])
    return jnp.dot(deep, jnp.concatenate(blocks, axis=0), preferred_element_type=jnp.float32)


def own_kernel(n_left, n_right, band, layers, first, last, *refs):
    place, keep = refs[:2]
    lefts = refs[2 : 2 + n_left]
    refs = refs[2 + n_left :]
    if first == 0:
        rights, refs = refs[:n_right], refs[n_right:]
        squares, sums, picks, panel, *refs = refs
    else:
        panel, before, squares, sums, picks, *refs = refs
    place_s, keep_s, product_a, product_b, sem, right_sem = refs
    copies = [
        pltpu.make_async_copy(place, place_s, sem.at[0]),
        pltpu.make_async_copy(keep, keep_s, sem.at[1]),
    ]
    if first == 0:
        me = lax.axis_index("row")
        depth = rights[0].shape[0]
        for k, right in enumerate(rights):
            at = pl.ds(pl.multiple_of((me ^ k) * depth, depth), depth)
            copies.append(pltpu.make_async_copy(right, panel.at[at, :], right_sem.at[k]))
    for copy in copies:
        copy.start()
    for copy in copies[2:]:
        copy.wait()
    bands = band // BS
    partial = [jnp.zeros((8, BS), jnp.float32) for _ in range(COLB)]
    for q in range(squares.shape[0] // band):
        product = (product_a, product_b)[q % 2]
        product[...] = product_of(lefts, panel, pl.ds(q * band, band))
        if q == 0:
            for copy in copies[:2]:
                copy.wait()
        for i in range(bands):
            row = (first + q) * bands + i
            for s in range(KOL):
                block = place_s[s, row]
                picked = product[pl.ds(i * BS, BS), pl.ds(pl.multiple_of(block * BS, BS), BS)]
                picks[pl.ds((q * bands + i) * KOL + s, 1), :] = jnp.full((1, BS), block, jnp.int32)
                square = picked * picked * keep_s[s, row].astype(jnp.float32)
                squares[pl.ds(q * band + i * BS, BS), pl.ds(s * BS, BS)] = square
                total = jnp.sum(square.reshape(BS // 8, 8, BS), axis=0)
                for c in range(COLB):
                    partial[c] = partial[c] + jnp.where(block == c, total, jnp.zeros_like(total))
    for c in range(COLB):
        total = jnp.sum(partial[c], axis=0, keepdims=True)
        if first:
            total = total + before[pl.ds(c, 1), :]
        sums[pl.ds(c, 1), :] = total


def own_squares(place, keep, lefts, rights, before, band, layers, first, last):
    rows = lefts[0].shape[0]
    inner = len(lefts) * BS
    out_shape = [
        jax.ShapeDtypeStruct((rows, OUT), jnp.float32),
        jax.ShapeDtypeStruct((COLB, BS), jnp.float32),
        jax.ShapeDtypeStruct((rows // BS * KOL, BS), jnp.int32),
    ]
    if first == 0:
        out_shape.append(jax.ShapeDtypeStruct((inner, TILE), jnp.bfloat16))
        more, specs = list(rights), [HBM] * len(rights)
    else:
        more, specs = list(before), [VMEM] * len(before)
    return call(
        functools.partial(own_kernel, len(lefts), len(rights), band, layers, first, last),
        out_shape,
        [HBM, HBM] + [VMEM] * len(lefts) + specs,
        [VMEM] * len(out_shape),
        [
            pltpu.SMEM(place.shape, jnp.int32),
            pltpu.SMEM(place.shape, jnp.int32),
            pltpu.VMEM((band, TILE), jnp.float32),
            pltpu.VMEM((band, TILE), jnp.float32),
            pltpu.SemaphoreType.DMA((2,)),
            pltpu.SemaphoreType.DMA((max(len(rights), 1),)),
        ],
        2 * rows * inner * TILE,
        2 * (rows + TILE) * inner + 4 * rows * OUT,
    )(*in_hbm(place, keep), *lefts, *more)


def row_scales(picks, sums, total_rows):
    scale = 1.0 / (sums / jnp.float32(total_rows) + 1e-6)
    rows = jnp.broadcast_to(scale[0:1, :], picks.shape)
    for c in range(1, COLB):
        rows = jnp.where(picks == c, scale[c : c + 1, :], rows)
    return rows


def scaled(squares, first, scales, target):
    for i in range(target.shape[0] // BS):
        for s in range(KOL):
            at = (pl.ds(first + i * BS, BS), pl.ds(s * BS, BS))
            to = (pl.ds(i * BS, BS), pl.ds(s * BS, BS))
            j = i * KOL + s
            target[to] = (squares[at] * scales[j : j + 1, :]).astype(target.dtype)


def scale_kernel(total_rows, chunk_bands, sums, other, meta, *refs):
    squares, picks = refs[:CHUNKS], refs[CHUNKS : 2 * CHUNKS]
    sent, own, message = refs[2 * CHUNKS :]
    layer = lax.axis_index("layer")
    whole = sums[...] + other[...]
    message[0:COLB, :] = whole
    message[COLB : COLB + 2 * KOL, :] = meta[...]
    band = own.shape[0]
    jobs = band // BS * KOL
    for part, target in ((1, sent), (0, own)):
        mine = layer ^ part
        for c in range(CHUNKS):

            @pl.when(mine // chunk_bands == c)
            def _():
                at = mine % chunk_bands
                chosen = picks[c][pl.ds(pl.multiple_of(at * jobs, jobs), jobs), :]
                scales = row_scales(chosen, whole, total_rows)
                scaled(squares[c], pl.multiple_of(at * band, band), scales, target)


def scale_own(sums, other, meta, squares, picks, band, total_rows):
    return call(
        functools.partial(scale_kernel, total_rows, squares[0].shape[0] // band),
        (
            jax.ShapeDtypeStruct((band, OUT), jnp.bfloat16),
            jax.ShapeDtypeStruct((band, OUT), jnp.bfloat16),
            jax.ShapeDtypeStruct((COLB + 2 * KOL, BS), jnp.float32),
        ),
        [VMEM] * (3 + 2 * CHUNKS),
        (VMEM, VMEM, VMEM),
        [],
        4 * band * OUT,
        12 * band * OUT,
    )(sums, other, meta, *squares, *picks)


def far_kernel(n_left, n_right, chunk_bands, *refs):
    chunks = [refs[c * n_left : (c + 1) * n_left] for c in range(CHUNKS)]
    refs = refs[CHUNKS * n_left :]
    rights = refs[:n_right]
    product, panel, right_sem = refs[n_right:]
    layer = lax.axis_index("layer")
    me = lax.axis_index("row")
    depth = rights[0].shape[0]
    copies = []
    for k, right in enumerate(rights):
        at = pl.ds(pl.multiple_of((me ^ k) * depth, depth), depth)
        copies.append(pltpu.make_async_copy(right, panel.at[at, :], right_sem.at[k]))
        copies[k].start()
    for copy in copies:
        copy.wait()
    band = product.shape[0]
    for c in range(CHUNKS):

        @pl.when(layer // chunk_bands == c)
        def _():
            at = pl.multiple_of((layer % chunk_bands) * band, band)
            product[...] = product_of(chunks[c], panel, pl.ds(at, band))


def far_product(chunks, rights, band):
    n_left = len(chunks[0])
    inner = n_left * BS
    lefts = [left for chunk in chunks for left in chunk]
    return call(
        functools.partial(far_kernel, n_left, len(rights), chunks[0][0].shape[0] // band),
        jax.ShapeDtypeStruct((band, TILE), jnp.float32),
        [VMEM] * (len(lefts) + len(rights)),
        VMEM,
        [
            pltpu.VMEM((inner, TILE), jnp.bfloat16),
            pltpu.SemaphoreType.DMA((len(rights),)),
        ],
        0,
        0,
    )(*lefts, *rights)


def last_kernel(total_rows, own, sent, *refs):
    products, messages = refs[0:2], refs[2:4]
    out, results, scales, message_s, sem, message_sem = refs[4], refs[5:7], refs[7], refs[8:10], refs[10], refs[11]
    layer = lax.axis_index("layer")
    loads = []
    for far in range(2):
        loads.append(pltpu.make_async_copy(messages[far], message_s[far], message_sem.at[far]))
        loads[far].start()
    copies = []

    def write(tile, bit):
        columns = pl.ds(pl.multiple_of((layer ^ bit) * OUT, OUT), OUT)
        copies.append(pltpu.make_async_copy(tile, out.at[:, columns], sem.at[bit]))
        copies[-1].start()

    write(own, 0)
    write(sent, 1)
    bands = own.shape[0] // BS
    for far in range(2):
        scales[far] = 1.0 / (messages[far][0:COLB, :] / jnp.float32(total_rows) + 1e-6)
    for far in range(2):
        loads[far].wait()
        for i in range(bands):
            for s in range(KOL):
                row = layer * bands + i
                block = message_s[far][COLB + s, row].astype(jnp.int32)
                weight = scales[far, pl.ds(block, 1), :] * message_s[far][COLB + KOL + s, row]
                columns = pl.ds(pl.multiple_of(block * BS, BS), BS)
                picked = products[far][pl.ds(i * BS, BS), columns]
                results[far][pl.ds(i * BS, BS), pl.ds(s * BS, BS)] = (picked * picked * weight).astype(
                    results[far].dtype
                )
        write(results[far], 2 + far)
    for copy in copies:
        copy.wait()


def last(own, sent, products, messages, layers, total_rows):
    band = own.shape[0]
    return call(
        functools.partial(last_kernel, total_rows),
        jax.ShapeDtypeStruct((band, layers * OUT), jnp.bfloat16),
        [VMEM] * 6,
        HBM,
        [
            pltpu.VMEM((band, OUT), jnp.bfloat16),
            pltpu.VMEM((band, OUT), jnp.bfloat16),
            pltpu.VMEM((2, COLB, BS), jnp.float32),
            pltpu.SMEM(messages[0].shape, jnp.float32),
            pltpu.SMEM(messages[0].shape, jnp.float32),
            pltpu.SemaphoreType.DMA((4,)),
            pltpu.SemaphoreType.DMA((2,)),
        ],
        4 * band * OUT,
        20 * band * OUT,
    )(own, sent, *products, *messages)


def shards(
    source_matrix_strip,
    target_matrix_strip,
    stored_tile_flag,
    target_place_tile_index,
    retained_target_flag,
):
    layers = lax.axis_size("layer")
    total_rows = source_matrix_strip.shape[0] * lax.axis_size("row")
    band = source_matrix_strip.shape[0] // layers
    place = target_place_tile_index.T
    keep = retained_target_flag.T
    half = lax.axis_size("col") // 2
    far = swap(target_matrix_strip, "layer", 2)
    masked, meta = mask_blocks(stored_tile_flag.T, source_matrix_strip, place, keep)
    across = [swap(piece, "col", half) for piece in masked]
    near = gather(target_matrix_strip, "row")
    across[0], _ = lax.optimization_barrier((across[0], far))
    chunks = [spread(m, "col", half) + spread(a, "col", half) for m, a in zip(masked, across)]
    opposite = swap(far, "layer", 1)
    far_pieces = gather(far, "row")
    squares, picks, sums, panel = [], [], None, None
    per = layers // CHUNKS
    for c in range(CHUNKS):
        before = (panel, sums)
        block, sums, pick, *rest = own_squares(place, keep, chunks[c], near, before, band, layers, c * per, c == CHUNKS - 1)
        squares.append(block)
        picks.append(pick)
        panel = rest[0] if rest else panel
    bit = lax.axis_size("row") // 2
    while bit > 1:
        sums = sums + swap(sums, "row", bit)
        bit //= 2
    sent, own, message = scale_own(sums, swap(sums, "row", 1), meta, squares, picks, band, total_rows)
    sent = swap(sent, "layer", 1)
    opposite, _, _ = lax.optimization_barrier((opposite, message, far_pieces))
    opposite_pieces = gather(opposite, "row")
    messages = [swap(message, "layer", 2), swap(message, "layer", 3)]
    products = [far_product(chunks, far_pieces, band), far_product(chunks, opposite_pieces, band)]
    return last(own, sent, products, messages, layers, total_rows)


def solution(mesh):
    placed = (
        P("row", "col"),
        P("row", ("col", "layer")),
        P("row", "col"),
        P("row", ("col", "layer")),
        P("row", ("col", "layer")),
    )
    return jax.shard_map(
        shards, mesh=mesh, in_specs=placed, out_specs=P(("row", "layer"), "col"), check_vma=False
    )
```

```python
import functools

import jax
import jax.numpy as jnp
from jax import lax
from jax.experimental import pallas as pl
from jax.experimental.pallas import tpu as pltpu
from jax.sharding import PartitionSpec as P

BS = 128
CHUNKS = 2
COLB = 4
KOL = 2
TILE = COLB * BS
OUT = KOL * BS
MASK_COST, OWN_COST, SCALE_COST, FAR_COST, TICK_COST = 0, 0, 0, 0, 10**11
VMEM_LIMIT = 12 * 1024 * 1024

HBM = pl.BlockSpec(memory_space=pltpu.HBM)
VMEM = pl.BlockSpec(memory_space=pltpu.VMEM)


def swap(value, axis, bit, name):
    count = lax.axis_size(axis)
    with jax.named_scope(name):
        return lax.ppermute(value, axis, [(i, i ^ bit) for i in range(count)])


def spread(piece, axis, count, name):
    pieces = {0: piece}
    bit = count // 2
    while bit:
        for k in list(pieces):
            pieces[k ^ bit] = swap(pieces[k], axis, bit, name)
        bit //= 2
    return [pieces[k] for k in range(count)]


def gather(piece, axis, name):
    return spread(piece, axis, lax.axis_size(axis), name)


def together(*values):
    return lax.optimization_barrier(values)


def in_hbm(*values):
    return [pltpu.with_memory_space_constraint(value, pltpu.HBM) for value in values]


def call(kernel, out_shape, in_specs, out_specs, scratch, cost, name, aliases=None):
    return pl.pallas_call(
        kernel,
        out_shape=out_shape,
        in_specs=in_specs,
        out_specs=out_specs,
        scratch_shapes=scratch,
        input_output_aliases=aliases or {},
        compiler_params=pltpu.CompilerParams(vmem_limit_bytes=VMEM_LIMIT),
        cost_estimate=pl.CostEstimate(flops=cost, bytes_accessed=0, transcendentals=0),
        name=name,
    )


def mask_kernel(flag, source, place, keep, masked, *refs):
    chunks, refs = refs[:CHUNKS], refs[CHUNKS:]
    meta, flag_s, panel, meta_v, sem, flag_sem, meta_sem = refs
    parts = sem.shape[0]
    rows = source.shape[0] // parts
    flag_copy = pltpu.make_async_copy(flag, flag_s, flag_sem)
    flag_copy.start()
    copies = []
    for c in range(parts):
        part = pl.ds(c * rows, rows)
        copies.append(pltpu.make_async_copy(source.at[part, :], panel.at[part, :], sem.at[c]))
        copies[c].start()
    metas = [
        pltpu.make_async_copy(place, meta_v.at[0:KOL, :], meta_sem.at[0]),
        pltpu.make_async_copy(keep, meta_v.at[KOL : 2 * KOL, :], meta_sem.at[1]),
    ]
    for copy in metas:
        copy.start()
    flag_copy.wait()
    for c in range(parts):
        copies[c].wait()
        for i in range(c * rows // BS, (c + 1) * rows // BS):
            at = pl.ds(i * BS, BS)
            block = panel[at, :]
            block = jnp.where(flag_s[0, i] != 0, block, jnp.zeros_like(block))
            masked[at, :] = block
            chunk, first = divmod(i * BS * CHUNKS, source.shape[0])
            chunks[chunk][pl.ds(first // CHUNKS, BS), :] = block
    for copy in metas:
        copy.wait()
    meta[...] = jnp.zeros_like(meta)
    meta[:, 0 : meta_v.shape[1]] = meta_v[...].astype(jnp.float32)


def mask_blocks(flag, source, place, keep):
    rows = source.shape[0]
    whole, *chunks, meta = call(
        mask_kernel,
        [jax.ShapeDtypeStruct(source.shape, source.dtype)]
        + [jax.ShapeDtypeStruct((rows // CHUNKS, BS), source.dtype)] * CHUNKS
        + [jax.ShapeDtypeStruct((2 * KOL, BS), jnp.float32)],
        [HBM] * 4,
        [VMEM] * (CHUNKS + 2),
        [
            pltpu.SMEM(flag.shape, jnp.int32),
            pltpu.VMEM(source.shape, source.dtype),
            pltpu.VMEM((2 * KOL, place.shape[1]), jnp.int32),
            pltpu.SemaphoreType.DMA((4,)),
            pltpu.SemaphoreType.DMA,
            pltpu.SemaphoreType.DMA((2,)),
        ],
        MASK_COST,
        "mask",
    )(*in_hbm(flag, source, place, keep))
    return whole, chunks, meta


def product_of(deep, right):
    me = lax.axis_index("col")
    blocks = []
    for k in range(deep.shape[1] // BS):
        place = pl.ds(pl.multiple_of((me ^ k) * BS, BS), BS)
        blocks.append(right[place, :])
    return jnp.dot(deep, jnp.concatenate(blocks, axis=0), preferred_element_type=jnp.float32)


def tick_kernel(before, after):
    after[...] = before[...]


def tick(value):
    return call(tick_kernel, jax.ShapeDtypeStruct(value.shape, value.dtype), [VMEM], VMEM, [], TICK_COST, "tick")(value)


def own_kernel(n_left, n_right, band, place, keep, *refs):
    earlies, refs = refs[:n_left], refs[n_left:]
    chunks = [refs[c * n_left : (c + 1) * n_left] for c in range(CHUNKS)]
    refs = refs[CHUNKS * n_left :]
    rights, refs = refs[:n_right], refs[n_right:]
    squares, sums, picks, panel, place_s, keep_s, product_a, product_b, sem, right_sem = refs
    me = lax.axis_index("row")
    depth = rights[0].shape[0]
    copies = [
        pltpu.make_async_copy(place, place_s, sem.at[0]),
        pltpu.make_async_copy(keep, keep_s, sem.at[1]),
    ]
    for k, right in enumerate(rights):
        at = pl.ds(pl.multiple_of((me ^ k) * depth, depth), depth)
        copies.append(pltpu.make_async_copy(right, panel.at[at, :], right_sem.at[k]))
    for copy in copies:
        copy.start()
    for copy in copies[2:]:
        copy.wait()
    bands = band // BS
    rows = squares.shape[0]
    partial = [jnp.zeros((8, BS), jnp.float32) for _ in range(COLB)]
    for q in range(rows // band):
        product = (product_a, product_b)[q % 2]
        chunk, first = divmod(q * band * CHUNKS, rows)
        deep = jnp.concatenate(
            [left[pl.ds(q * band, band), :] for left in earlies]
            + [left[pl.ds(first // CHUNKS, band), :] for left in chunks[chunk]],
            axis=1,
        )
        product[...] = product_of(deep, panel)
        if q == 0:
            for copy in copies[:2]:
                copy.wait()
        for i in range(bands):
            for s in range(KOL):
                row = q * bands + i
                block = place_s[s, row]
                picks[pl.ds(row * KOL + s, 1), :] = jnp.full((1, BS), block, jnp.int32)
                columns = pl.ds(pl.multiple_of(block * BS, BS), BS)
                picked = product[pl.ds(i * BS, BS), columns]
                square = picked * picked * keep_s[s, row].astype(jnp.float32)
                squares[pl.ds(row * BS, BS), pl.ds(s * BS, BS)] = square
                total = jnp.sum(square.reshape(BS // 8, 8, BS), axis=0)
                for c in range(COLB):
                    partial[c] = partial[c] + jnp.where(block == c, total, jnp.zeros_like(total))
    for c in range(COLB):
        sums[pl.ds(c, 1), :] = jnp.sum(partial[c], axis=0, keepdims=True)


def own_squares(place, keep, earlies, chunks, rights, band):
    rows = earlies[0].shape[0]
    inner = rights[0].shape[0] * len(rights)
    lefts = list(earlies) + [left for chunk in chunks for left in chunk]
    return call(
        functools.partial(own_kernel, len(earlies), len(rights), band),
        (
            jax.ShapeDtypeStruct((rows, OUT), jnp.float32),
            jax.ShapeDtypeStruct((COLB, BS), jnp.float32),
            jax.ShapeDtypeStruct((rows // BS * KOL, BS), jnp.int32),
        ),
        [HBM, HBM] + [VMEM] * len(lefts) + [HBM] + [pl.BlockSpec(memory_space=pl.ANY)] * (len(rights) - 1),
        (VMEM, VMEM, VMEM),
        [
            pltpu.VMEM((inner, TILE), jnp.bfloat16),
            pltpu.SMEM(place.shape, jnp.int32),
            pltpu.SMEM(place.shape, jnp.int32),
            pltpu.VMEM((band, TILE), jnp.float32),
            pltpu.VMEM((band, TILE), jnp.float32),
            pltpu.SemaphoreType.DMA((2,)),
            pltpu.SemaphoreType.DMA((len(rights),)),
        ],
        OWN_COST,
        "own",
    )(*in_hbm(place, keep), *lefts, *in_hbm(rights[0]), *rights[1:])


def row_scales(picks, sums, total_rows):
    scale = 1.0 / (sums / jnp.float32(total_rows) + 1e-6)
    rows = jnp.broadcast_to(scale[0:1, :], picks.shape)
    for c in range(1, COLB):
        rows = jnp.where(picks == c, scale[c : c + 1, :], rows)
    return rows


def scaled(squares, first, scales, target):
    for i in range(target.shape[0] // BS):
        for s in range(KOL):
            at = (pl.ds(first + i * BS, BS), pl.ds(s * BS, BS))
            to = (pl.ds(i * BS, BS), pl.ds(s * BS, BS))
            j = i * KOL + s
            target[to] = (squares[at] * scales[j : j + 1, :]).astype(target.dtype)


def scale_kernel(total_rows, sums, other, meta, squares, picks, sent, own, message):
    layer = lax.axis_index("layer")
    whole = sums[...] + other[...]
    message[0:COLB, :] = whole
    message[COLB : COLB + 2 * KOL, :] = meta[...]
    band = own.shape[0]
    jobs = band // BS * KOL
    for part, target in ((1, sent), (0, own)):
        mine = layer ^ part
        chosen = picks[pl.ds(pl.multiple_of(mine * jobs, jobs), jobs), :]
        scales = row_scales(chosen, whole, total_rows)
        scaled(squares, pl.multiple_of(mine * band, band), scales, target)


def scale_own(sums, other, meta, squares, picks, band, total_rows):
    return call(
        functools.partial(scale_kernel, total_rows),
        (
            jax.ShapeDtypeStruct((band, OUT), jnp.bfloat16),
            jax.ShapeDtypeStruct((band, OUT), jnp.bfloat16),
            jax.ShapeDtypeStruct((COLB + 2 * KOL, BS), jnp.float32),
        ),
        [VMEM] * 5,
        (VMEM, VMEM, VMEM),
        [],
        SCALE_COST,
        "scale",
    )(sums, other, meta, squares, picks)


def far_tile(message, scales, rights, deep, product, message_s, copy, total_rows, result):
    layer = lax.axis_index("layer")
    me = lax.axis_index("row")
    scales[...] = 1.0 / (message[0:COLB, :] / jnp.float32(total_rows) + 1e-6)
    depth = rights[0].shape[0]
    whole = None
    for k, right in enumerate(rights):
        columns = pl.ds(pl.multiple_of((me ^ k) * depth, depth), depth)
        term = jnp.dot(deep[:, columns], right[...], preferred_element_type=jnp.float32)
        whole = term if whole is None else whole + term
    product[...] = whole
    copy.wait()
    bands = deep.shape[0] // BS
    for i in range(bands):
        for s in range(KOL):
            row = layer * bands + i
            block = message_s[COLB + s, row].astype(jnp.int32)
            weight = scales[pl.ds(block, 1), :] * message_s[COLB + KOL + s, row]
            picked = product[pl.ds(i * BS, BS), pl.ds(pl.multiple_of(block * BS, BS), BS)]
            result[pl.ds(i * BS, BS), pl.ds(s * BS, BS)] = (picked * picked * weight).astype(result.dtype)


def tile_columns(bit):
    return pl.ds(pl.multiple_of((lax.axis_index("layer") ^ bit) * OUT, OUT), OUT)


def far_kernel(n_left, n_right, total_rows, message, own, *refs):
    earlies, refs = refs[:n_left], refs[n_left:]
    chunks = [refs[c * n_left : (c + 1) * n_left] for c in range(CHUNKS)]
    refs = refs[CHUNKS * n_left :]
    rights, refs = refs[:n_right], refs[n_right:]
    out, deep, scales, product, result, message_s, message_sem, sem = refs
    layer = lax.axis_index("layer")
    me = lax.axis_index("col")
    load = pltpu.make_async_copy(message, message_s, message_sem)
    load.start()
    own_copy = pltpu.make_async_copy(own, out.at[:, tile_columns(0)], sem.at[0])
    own_copy.start()
    band = deep.shape[0]
    own_rows = pl.ds(pl.multiple_of(layer * band, band), band)
    for k, left in enumerate(earlies):
        deep[:, pl.ds(pl.multiple_of((me ^ k) * BS, BS), BS)] = left[own_rows, :]
    per = chunks[0][0].shape[0] // band
    for c in range(CHUNKS):

        @pl.when(layer // per == c)
        def _():
            rows = pl.ds(pl.multiple_of((layer % per) * band, band), band)
            for k, left in enumerate(chunks[c]):
                deep[:, pl.ds(pl.multiple_of((me ^ (n_left + k)) * BS, BS), BS)] = left[rows, :]

    far_tile(message, scales, rights, deep, product, message_s, load, total_rows, result)
    far_copy = pltpu.make_async_copy(result, out.at[:, tile_columns(2)], sem.at[1])
    far_copy.start()
    own_copy.wait()
    far_copy.wait()


def far_tiles(message, own, earlies, chunks, rights, layers, total_rows):
    lefts = list(earlies) + [left for chunk in chunks for left in chunk]
    inner = 2 * len(earlies) * BS
    band = own.shape[0]
    return call(
        functools.partial(far_kernel, len(earlies), len(rights), total_rows),
        (
            jax.ShapeDtypeStruct((band, layers * OUT), jnp.bfloat16),
            jax.ShapeDtypeStruct((band, inner), jnp.bfloat16),
        ),
        [VMEM] * (2 + len(lefts) + len(rights)),
        (HBM, VMEM),
        [
            pltpu.VMEM((COLB, BS), jnp.float32),
            pltpu.VMEM((band, TILE), jnp.float32),
            pltpu.VMEM((band, OUT), jnp.bfloat16),
            pltpu.SMEM(message.shape, jnp.float32),
            pltpu.SemaphoreType.DMA,
            pltpu.SemaphoreType.DMA((2,)),
        ],
        FAR_COST,
        "far",
    )(message, own, *lefts, *rights)


def last_kernel(n_right, total_rows, message, sent, deep, *refs):
    rights, refs = refs[:n_right], refs[n_right:]
    _, out, scales, product, result, message_s, message_sem, sem = refs
    load = pltpu.make_async_copy(message, message_s, message_sem)
    load.start()
    sent_copy = pltpu.make_async_copy(sent, out.at[:, tile_columns(1)], sem.at[0])
    sent_copy.start()
    far_tile(message, scales, rights, deep, product, message_s, load, total_rows, result)
    far_copy = pltpu.make_async_copy(result, out.at[:, tile_columns(3)], sem.at[1])
    far_copy.start()
    sent_copy.wait()
    far_copy.wait()


def last_tiles(message, sent, deep, rights, out, total_rows):
    band = deep.shape[0]
    return call(
        functools.partial(last_kernel, len(rights), total_rows),
        jax.ShapeDtypeStruct(out.shape, out.dtype),
        [VMEM] * (3 + len(rights)) + [HBM],
        HBM,
        [
            pltpu.VMEM((COLB, BS), jnp.float32),
            pltpu.VMEM((band, TILE), jnp.float32),
            pltpu.VMEM((band, OUT), jnp.bfloat16),
            pltpu.SMEM(message.shape, jnp.float32),
            pltpu.SemaphoreType.DMA,
            pltpu.SemaphoreType.DMA((2,)),
        ],
        FAR_COST,
        "last",
        {3 + len(rights): 0},
    )(message, sent, deep, *rights, out)


def shards(
    source_matrix_strip,
    target_matrix_strip,
    stored_tile_flag,
    target_place_tile_index,
    retained_target_flag,
):
    layers = lax.axis_size("layer")
    total_rows = source_matrix_strip.shape[0] * lax.axis_size("row")
    band = source_matrix_strip.shape[0] // layers
    place = target_place_tile_index.T
    keep = retained_target_flag.T
    half = lax.axis_size("col") // 2
    whole, masked, meta = mask_blocks(stored_tile_flag.T, source_matrix_strip, place, keep)
    target, meta = together(target_matrix_strip, meta)
    across = [swap(piece, "col", half, "left_across") for piece in masked]
    far = swap(target, "layer", 2, "right_far")
    near = gather(target, "row", "right_near")
    earlies = spread(whole, "col", half, "left_early")
    far, across[0] = together(far, across[0])
    lates = [spread(piece, "col", half, "left_late") for piece in across]
    opposite = swap(far, "layer", 1, "right_opposite")
    far_pieces = gather(far, "row", "right_far_row")
    squares, sums, picks = own_squares(place, keep, earlies, lates, near, band)
    bit = lax.axis_size("row") // 2
    while bit > 1:
        sums = sums + swap(sums, "row", bit, "sums_row")
        bit //= 2
    other = swap(sums, "row", 1, "sums_row")
    far_pieces[-1], opposite, other = together(far_pieces[-1], opposite, other)
    sent, own, message = scale_own(sums, other, meta, squares, picks, band, total_rows)
    sent = swap(sent, "layer", 1, "sent")
    opposite_pieces = gather(opposite, "row", "right_opposite_row")
    messages = [swap(message, "layer", 2, "sums_far"), swap(message, "layer", 3, "sums_opposite")]
    out, deep = far_tiles(messages[0], own, earlies, lates, far_pieces, layers, total_rows)
    return last_tiles(messages[1], sent, deep, opposite_pieces, out, total_rows)


def solution(mesh):
    placed = (
        P("row", "col"),
        P("row", ("col", "layer")),
        P("row", "col"),
        P("row", ("col", "layer")),
        P("row", ("col", "layer")),
    )
    return jax.shard_map(
        shards, mesh=mesh, in_specs=placed, out_specs=P(("row", "layer"), "col"), check_vma=False
    )
```

```python
import functools

import jax
import jax.numpy as jnp
from jax import lax
from jax.experimental import pallas as pl
from jax.experimental.pallas import tpu as pltpu
from jax.sharding import PartitionSpec as P

BS = 128
CHUNKS = 2
COLB = 4
KOL = 2
TILE = COLB * BS
OUT = KOL * BS
MASK_COST, OWN_COST, SCALE_COST, FAR_COST, TICK_COST = 0, 0, 0, 0, 10**11
VMEM_LIMIT = 12 * 1024 * 1024

HBM = pl.BlockSpec(memory_space=pltpu.HBM)
VMEM = pl.BlockSpec(memory_space=pltpu.VMEM)


def swap(value, axis, bit, name):
    count = lax.axis_size(axis)
    with jax.named_scope(name):
        return lax.ppermute(value, axis, [(i, i ^ bit) for i in range(count)])


def spread(piece, axis, count, name):
    pieces = {0: piece}
    bit = count // 2
    while bit:
        for k in list(pieces):
            pieces[k ^ bit] = swap(pieces[k], axis, bit, name)
        bit //= 2
    return [pieces[k] for k in range(count)]


def gather(piece, axis, name):
    return spread(piece, axis, lax.axis_size(axis), name)


def together(*values):
    return lax.optimization_barrier(values)


def in_hbm(*values):
    return [pltpu.with_memory_space_constraint(value, pltpu.HBM) for value in values]


def call(kernel, out_shape, in_specs, out_specs, scratch, cost, name, aliases=None):
    return pl.pallas_call(
        kernel,
        out_shape=out_shape,
        in_specs=in_specs,
        out_specs=out_specs,
        scratch_shapes=scratch,
        input_output_aliases=aliases or {},
        compiler_params=pltpu.CompilerParams(vmem_limit_bytes=VMEM_LIMIT),
        cost_estimate=pl.CostEstimate(flops=cost, bytes_accessed=0, transcendentals=0),
        name=name,
    )


def mask_kernel(flag, source, place, keep, masked, *refs):
    chunks, refs = refs[:CHUNKS], refs[CHUNKS:]
    meta, flag_s, panel, meta_v, sem, flag_sem, meta_sem = refs
    parts = sem.shape[0]
    rows = source.shape[0] // parts
    flag_copy = pltpu.make_async_copy(flag, flag_s, flag_sem)
    flag_copy.start()
    copies = []
    for c in range(parts):
        part = pl.ds(c * rows, rows)
        copies.append(pltpu.make_async_copy(source.at[part, :], panel.at[part, :], sem.at[c]))
        copies[c].start()
    metas = [
        pltpu.make_async_copy(place, meta_v.at[0:KOL, :], meta_sem.at[0]),
        pltpu.make_async_copy(keep, meta_v.at[KOL : 2 * KOL, :], meta_sem.at[1]),
    ]
    for copy in metas:
        copy.start()
    flag_copy.wait()
    for c in range(parts):
        copies[c].wait()
        for i in range(c * rows // BS, (c + 1) * rows // BS):
            at = pl.ds(i * BS, BS)
            block = panel[at, :]
            block = jnp.where(flag_s[0, i] != 0, block, jnp.zeros_like(block))
            masked[at, :] = block
            chunk, first = divmod(i * BS * CHUNKS, source.shape[0])
            chunks[chunk][pl.ds(first // CHUNKS, BS), :] = block
    for copy in metas:
        copy.wait()
    meta[...] = jnp.zeros_like(meta)
    meta[:, 0 : meta_v.shape[1]] = meta_v[...].astype(jnp.float32)


def mask_blocks(flag, source, place, keep):
    rows = source.shape[0]
    whole, *chunks, meta = call(
        mask_kernel,
        [jax.ShapeDtypeStruct(source.shape, source.dtype)]
        + [jax.ShapeDtypeStruct((rows // CHUNKS, BS), source.dtype)] * CHUNKS
        + [jax.ShapeDtypeStruct((2 * KOL, BS), jnp.float32)],
        [HBM] * 4,
        [VMEM] * (CHUNKS + 2),
        [
            pltpu.SMEM(flag.shape, jnp.int32),
            pltpu.VMEM(source.shape, source.dtype),
            pltpu.VMEM((2 * KOL, place.shape[1]), jnp.int32),
            pltpu.SemaphoreType.DMA((4,)),
            pltpu.SemaphoreType.DMA,
            pltpu.SemaphoreType.DMA((2,)),
        ],
        MASK_COST,
        "mask",
    )(*in_hbm(flag, source, place, keep))
    return whole, chunks, meta


def product_of(deep, right):
    me = lax.axis_index("col")
    blocks = []
    for k in range(deep.shape[1] // BS):
        place = pl.ds(pl.multiple_of((me ^ k) * BS, BS), BS)
        blocks.append(right[place, :])
    return jnp.dot(deep, jnp.concatenate(blocks, axis=0), preferred_element_type=jnp.float32)


def tick_kernel(before, after):
    after[...] = before[...]


def tick(value):
    return call(tick_kernel, jax.ShapeDtypeStruct(value.shape, value.dtype), [VMEM], VMEM, [], TICK_COST, "tick")(value)


def own_kernel(n_left, n_right, band, place, keep, *refs):
    earlies, refs = refs[:n_left], refs[n_left:]
    chunks = [refs[c * n_left : (c + 1) * n_left] for c in range(CHUNKS)]
    refs = refs[CHUNKS * n_left :]
    rights, refs = refs[:n_right], refs[n_right:]
    squares, sums, picks, panel, place_s, keep_s, product_a, product_b, sem, right_sem = refs
    me = lax.axis_index("row")
    depth = rights[0].shape[0]
    copies = [
        pltpu.make_async_copy(place, place_s, sem.at[0]),
        pltpu.make_async_copy(keep, keep_s, sem.at[1]),
    ]
    for k, right in enumerate(rights):
        at = pl.ds(pl.multiple_of((me ^ k) * depth, depth), depth)
        copies.append(pltpu.make_async_copy(right, panel.at[at, :], right_sem.at[k]))
    for copy in copies:
        copy.start()
    for copy in copies[2:]:
        copy.wait()
    bands = band // BS
    rows = squares.shape[0]
    partial = [jnp.zeros((8, BS), jnp.float32) for _ in range(COLB)]
    for q in range(rows // band):
        product = (product_a, product_b)[q % 2]
        chunk, first = divmod(q * band * CHUNKS, rows)
        deep = jnp.concatenate(
            [left[pl.ds(q * band, band), :] for left in earlies]
            + [left[pl.ds(first // CHUNKS, band), :] for left in chunks[chunk]],
            axis=1,
        )
        product[...] = product_of(deep, panel)
        if q == 0:
            for copy in copies[:2]:
                copy.wait()
        for i in range(bands):
            for s in range(KOL):
                row = q * bands + i
                block = place_s[s, row]
                picks[pl.ds(row * KOL + s, 1), :] = jnp.full((1, BS), block, jnp.int32)
                columns = pl.ds(pl.multiple_of(block * BS, BS), BS)
                picked = product[pl.ds(i * BS, BS), columns]
                square = picked * picked * keep_s[s, row].astype(jnp.float32)
                squares[pl.ds(row * BS, BS), pl.ds(s * BS, BS)] = square
                total = jnp.sum(square.reshape(BS // 8, 8, BS), axis=0)
                for c in range(COLB):
                    partial[c] = partial[c] + jnp.where(block == c, total, jnp.zeros_like(total))
    for c in range(COLB):
        sums[pl.ds(c, 1), :] = jnp.sum(partial[c], axis=0, keepdims=True)


def own_squares(place, keep, earlies, chunks, rights, band):
    rows = earlies[0].shape[0]
    inner = rights[0].shape[0] * len(rights)
    lefts = list(earlies) + [left for chunk in chunks for left in chunk]
    return call(
        functools.partial(own_kernel, len(earlies), len(rights), band),
        (
            jax.ShapeDtypeStruct((rows, OUT), jnp.float32),
            jax.ShapeDtypeStruct((COLB, BS), jnp.float32),
            jax.ShapeDtypeStruct((rows // BS * KOL, BS), jnp.int32),
        ),
        [HBM, HBM] + [VMEM] * len(lefts) + [HBM] + [pl.BlockSpec(memory_space=pl.ANY)] * (len(rights) - 1),
        (VMEM, VMEM, VMEM),
        [
            pltpu.VMEM((inner, TILE), jnp.bfloat16),
            pltpu.SMEM(place.shape, jnp.int32),
            pltpu.SMEM(place.shape, jnp.int32),
            pltpu.VMEM((band, TILE), jnp.float32),
            pltpu.VMEM((band, TILE), jnp.float32),
            pltpu.SemaphoreType.DMA((2,)),
            pltpu.SemaphoreType.DMA((len(rights),)),
        ],
        OWN_COST,
        "own",
    )(*in_hbm(place, keep), *lefts, *in_hbm(rights[0]), *rights[1:])


def row_scales(picks, sums, total_rows):
    scale = 1.0 / (sums / jnp.float32(total_rows) + 1e-6)
    rows = jnp.broadcast_to(scale[0:1, :], picks.shape)
    for c in range(1, COLB):
        rows = jnp.where(picks == c, scale[c : c + 1, :], rows)
    return rows


def scaled(squares, first, scales, target):
    for i in range(target.shape[0] // BS):
        for s in range(KOL):
            at = (pl.ds(first + i * BS, BS), pl.ds(s * BS, BS))
            to = (pl.ds(i * BS, BS), pl.ds(s * BS, BS))
            j = i * KOL + s
            target[to] = (squares[at] * scales[j : j + 1, :]).astype(target.dtype)


def scale_kernel(total_rows, sums, other, meta, squares, picks, sent, own, message):
    layer = lax.axis_index("layer")
    whole = sums[...] + other[...]
    message[0:COLB, :] = whole
    message[COLB : COLB + 2 * KOL, :] = meta[...]
    band = own.shape[0]
    jobs = band // BS * KOL
    for part, target in ((1, sent), (0, own)):
        mine = layer ^ part
        chosen = picks[pl.ds(pl.multiple_of(mine * jobs, jobs), jobs), :]
        scales = row_scales(chosen, whole, total_rows)
        scaled(squares, pl.multiple_of(mine * band, band), scales, target)


def scale_own(sums, other, meta, squares, picks, band, total_rows):
    return call(
        functools.partial(scale_kernel, total_rows),
        (
            jax.ShapeDtypeStruct((band, OUT), jnp.bfloat16),
            jax.ShapeDtypeStruct((band, OUT), jnp.bfloat16),
            jax.ShapeDtypeStruct((COLB + 2 * KOL, BS), jnp.float32),
        ),
        [VMEM] * 5,
        (VMEM, VMEM, VMEM),
        [],
        SCALE_COST,
        "scale",
    )(sums, other, meta, squares, picks)


def far_tile(message, scales, rights, deep, product, message_s, copy, total_rows, result):
    layer = lax.axis_index("layer")
    me = lax.axis_index("row")
    scales[...] = 1.0 / (message[0:COLB, :] / jnp.float32(total_rows) + 1e-6)
    depth = rights[0].shape[0]
    whole = None
    for k, right in enumerate(rights):
        columns = pl.ds(pl.multiple_of((me ^ k) * depth, depth), depth)
        term = jnp.dot(deep[:, columns], right[...], preferred_element_type=jnp.float32)
        whole = term if whole is None else whole + term
    product[...] = whole
    copy.wait()
    bands = deep.shape[0] // BS
    for i in range(bands):
        for s in range(KOL):
            row = layer * bands + i
            block = message_s[COLB + s, row].astype(jnp.int32)
            weight = scales[pl.ds(block, 1), :] * message_s[COLB + KOL + s, row]
            picked = product[pl.ds(i * BS, BS), pl.ds(pl.multiple_of(block * BS, BS), BS)]
            result[pl.ds(i * BS, BS), pl.ds(s * BS, BS)] = (picked * picked * weight).astype(result.dtype)


def tile_columns(bit):
    return pl.ds(pl.multiple_of((lax.axis_index("layer") ^ bit) * OUT, OUT), OUT)


def far_kernel(n_left, n_right, total_rows, message, own, *refs):
    earlies, refs = refs[:n_left], refs[n_left:]
    chunks = [refs[c * n_left : (c + 1) * n_left] for c in range(CHUNKS)]
    refs = refs[CHUNKS * n_left :]
    rights, refs = refs[:n_right], refs[n_right:]
    out, deep, scales, product, result, message_s, message_sem, sem = refs
    layer = lax.axis_index("layer")
    me = lax.axis_index("col")
    load = pltpu.make_async_copy(message, message_s, message_sem)
    load.start()
    own_copy = pltpu.make_async_copy(own, out.at[:, tile_columns(0)], sem.at[0])
    own_copy.start()
    band = deep.shape[0]
    own_rows = pl.ds(pl.multiple_of(layer * band, band), band)
    for k, left in enumerate(earlies):
        deep[:, pl.ds(pl.multiple_of((me ^ k) * BS, BS), BS)] = left[own_rows, :]
    per = chunks[0][0].shape[0] // band
    for c in range(CHUNKS):

        @pl.when(layer // per == c)
        def _():
            rows = pl.ds(pl.multiple_of((layer % per) * band, band), band)
            for k, left in enumerate(chunks[c]):
                deep[:, pl.ds(pl.multiple_of((me ^ (n_left + k)) * BS, BS), BS)] = left[rows, :]

    far_tile(message, scales, rights, deep, product, message_s, load, total_rows, result)
    far_copy = pltpu.make_async_copy(result, out.at[:, tile_columns(2)], sem.at[1])
    far_copy.start()
    own_copy.wait()
    far_copy.wait()


def far_tiles(message, own, earlies, chunks, rights, layers, total_rows):
    lefts = list(earlies) + [left for chunk in chunks for left in chunk]
    inner = 2 * len(earlies) * BS
    band = own.shape[0]
    return call(
        functools.partial(far_kernel, len(earlies), len(rights), total_rows),
        (
            jax.ShapeDtypeStruct((band, layers * OUT), jnp.bfloat16),
            jax.ShapeDtypeStruct((band, inner), jnp.bfloat16),
        ),
        [VMEM] * (2 + len(lefts) + len(rights)),
        (HBM, VMEM),
        [
            pltpu.VMEM((COLB, BS), jnp.float32),
            pltpu.VMEM((band, TILE), jnp.float32),
            pltpu.VMEM((band, OUT), jnp.bfloat16),
            pltpu.SMEM(message.shape, jnp.float32),
            pltpu.SemaphoreType.DMA,
            pltpu.SemaphoreType.DMA((2,)),
        ],
        FAR_COST,
        "far",
    )(message, own, *lefts, *rights)


def last_kernel(n_right, total_rows, message, sent, deep, *refs):
    rights, refs = refs[:n_right], refs[n_right:]
    _, out, scales, product, result, message_s, message_sem, sem = refs
    load = pltpu.make_async_copy(message, message_s, message_sem)
    load.start()
    sent_copy = pltpu.make_async_copy(sent, out.at[:, tile_columns(1)], sem.at[0])
    sent_copy.start()
    far_tile(message, scales, rights, deep, product, message_s, load, total_rows, result)
    far_copy = pltpu.make_async_copy(result, out.at[:, tile_columns(3)], sem.at[1])
    far_copy.start()
    sent_copy.wait()
    far_copy.wait()


def last_tiles(message, sent, deep, rights, out, total_rows):
    band = deep.shape[0]
    return call(
        functools.partial(last_kernel, len(rights), total_rows),
        jax.ShapeDtypeStruct(out.shape, out.dtype),
        [VMEM] * (3 + len(rights)) + [HBM],
        HBM,
        [
            pltpu.VMEM((COLB, BS), jnp.float32),
            pltpu.VMEM((band, TILE), jnp.float32),
            pltpu.VMEM((band, OUT), jnp.bfloat16),
            pltpu.SMEM(message.shape, jnp.float32),
            pltpu.SemaphoreType.DMA,
            pltpu.SemaphoreType.DMA((2,)),
        ],
        FAR_COST,
        "last",
        {3 + len(rights): 0},
    )(message, sent, deep, *rights, out)


def shards(
    source_matrix_strip,
    target_matrix_strip,
    stored_tile_flag,
    target_place_tile_index,
    retained_target_flag,
):
    layers = lax.axis_size("layer")
    total_rows = source_matrix_strip.shape[0] * lax.axis_size("row")
    band = source_matrix_strip.shape[0] // layers
    place = target_place_tile_index.T
    keep = retained_target_flag.T
    half = lax.axis_size("col") // 2
    whole, masked, meta = mask_blocks(stored_tile_flag.T, source_matrix_strip, place, keep)
    target = target_matrix_strip
    across = [swap(piece, "col", half, "left_across") for piece in masked]
    far = swap(target, "layer", 2, "right_far")
    near = gather(target, "row", "right_near")
    earlies = spread(whole, "col", half, "left_early")
    far, across[0] = together(far, across[0])
    lates = [spread(piece, "col", half, "left_late") for piece in across]
    opposite = swap(far, "layer", 1, "right_opposite")
    far_pieces = gather(far, "row", "right_far_row")
    squares, sums, picks = own_squares(place, keep, earlies, lates, near, band)
    bit = lax.axis_size("row") // 2
    while bit > 1:
        sums = sums + swap(sums, "row", bit, "sums_row")
        bit //= 2
    other = swap(sums, "row", 1, "sums_row")
    far_pieces[-1], opposite, other = together(far_pieces[-1], opposite, other)
    sent, own, message = scale_own(sums, other, meta, squares, picks, band, total_rows)
    sent = swap(sent, "layer", 1, "sent")
    opposite_pieces = gather(opposite, "row", "right_opposite_row")
    messages = [swap(message, "layer", 2, "sums_far"), swap(message, "layer", 3, "sums_opposite")]
    out, deep = far_tiles(messages[0], own, earlies, lates, far_pieces, layers, total_rows)
    return last_tiles(messages[1], sent, deep, opposite_pieces, out, total_rows)


def solution(mesh):
    placed = (
        P("row", "col"),
        P("row", ("col", "layer")),
        P("row", "col"),
        P("row", ("col", "layer")),
        P("row", ("col", "layer")),
    )
    return jax.shard_map(
        shards, mesh=mesh, in_specs=placed, out_specs=P(("row", "layer"), "col"), check_vma=False
    )
```

```python
import functools

import jax
import jax.numpy as jnp
from jax import lax
from jax.experimental import pallas as pl
from jax.experimental.pallas import tpu as pltpu
from jax.sharding import PartitionSpec as P

BS = 128
CHUNKS = 2
COLB = 4
KOL = 2
TILE = COLB * BS
OUT = KOL * BS
MASK_COST, OWN_COST, SCALE_COST, FAR_COST, TICK_COST = 0, 0, 0, 0, 10**11
VMEM_LIMIT = 12 * 1024 * 1024

HBM = pl.BlockSpec(memory_space=pltpu.HBM)
VMEM = pl.BlockSpec(memory_space=pltpu.VMEM)


def swap(value, axis, bit, name):
    count = lax.axis_size(axis)
    with jax.named_scope(name):
        return lax.ppermute(value, axis, [(i, i ^ bit) for i in range(count)])


def spread(piece, axis, count, name):
    pieces = {0: piece}
    bit = count // 2
    while bit:
        for k in list(pieces):
            pieces[k ^ bit] = swap(pieces[k], axis, bit, name)
        bit //= 2
    return [pieces[k] for k in range(count)]


def gather(piece, axis, name):
    return spread(piece, axis, lax.axis_size(axis), name)


def together(*values):
    return lax.optimization_barrier(values)


def in_hbm(*values):
    return [pltpu.with_memory_space_constraint(value, pltpu.HBM) for value in values]


def call(kernel, out_shape, in_specs, out_specs, scratch, cost, name, aliases=None):
    return pl.pallas_call(
        kernel,
        out_shape=out_shape,
        in_specs=in_specs,
        out_specs=out_specs,
        scratch_shapes=scratch,
        input_output_aliases=aliases or {},
        compiler_params=pltpu.CompilerParams(vmem_limit_bytes=VMEM_LIMIT),
        cost_estimate=pl.CostEstimate(flops=cost, bytes_accessed=0, transcendentals=0),
        name=name,
    )


def mask_kernel(flag, source, place, keep, masked, *refs):
    chunks, refs = refs[:CHUNKS], refs[CHUNKS:]
    meta, flag_s, panel, meta_v, sem, flag_sem, meta_sem = refs
    parts = sem.shape[0]
    rows = source.shape[0] // parts
    flag_copy = pltpu.make_async_copy(flag, flag_s, flag_sem)
    flag_copy.start()
    copies = []
    for c in range(parts):
        part = pl.ds(c * rows, rows)
        copies.append(pltpu.make_async_copy(source.at[part, :], panel.at[part, :], sem.at[c]))
        copies[c].start()
    metas = [
        pltpu.make_async_copy(place, meta_v.at[0:KOL, :], meta_sem.at[0]),
        pltpu.make_async_copy(keep, meta_v.at[KOL : 2 * KOL, :], meta_sem.at[1]),
    ]
    for copy in metas:
        copy.start()
    flag_copy.wait()
    for c in range(parts):
        copies[c].wait()
        for i in range(c * rows // BS, (c + 1) * rows // BS):
            at = pl.ds(i * BS, BS)
            block = panel[at, :]
            block = jnp.where(flag_s[0, i] != 0, block, jnp.zeros_like(block))
            masked[at, :] = block
            chunk, first = divmod(i * BS * CHUNKS, source.shape[0])
            chunks[chunk][pl.ds(first // CHUNKS, BS), :] = block
    for copy in metas:
        copy.wait()
    meta[...] = jnp.zeros_like(meta)
    meta[:, 0 : meta_v.shape[1]] = meta_v[...].astype(jnp.float32)


def mask_blocks(flag, source, place, keep):
    rows = source.shape[0]
    whole, *chunks, meta = call(
        mask_kernel,
        [jax.ShapeDtypeStruct(source.shape, source.dtype)]
        + [jax.ShapeDtypeStruct((rows // CHUNKS, BS), source.dtype)] * CHUNKS
        + [jax.ShapeDtypeStruct((2 * KOL, BS), jnp.float32)],
        [HBM] * 4,
        [VMEM] * (CHUNKS + 2),
        [
            pltpu.SMEM(flag.shape, jnp.int32),
            pltpu.VMEM(source.shape, source.dtype),
            pltpu.VMEM((2 * KOL, place.shape[1]), jnp.int32),
            pltpu.SemaphoreType.DMA((4,)),
            pltpu.SemaphoreType.DMA,
            pltpu.SemaphoreType.DMA((2,)),
        ],
        MASK_COST,
        "mask",
    )(*in_hbm(flag, source, place, keep))
    return whole, chunks, meta


def product_of(deep, right):
    me = lax.axis_index("col")
    blocks = []
    for k in range(deep.shape[1] // BS):
        place = pl.ds(pl.multiple_of((me ^ k) * BS, BS), BS)
        blocks.append(right[place, :])
    return jnp.dot(deep, jnp.concatenate(blocks, axis=0), preferred_element_type=jnp.float32)


def tick_kernel(before, after):
    after[...] = before[...]


def tick(value):
    return call(tick_kernel, jax.ShapeDtypeStruct(value.shape, value.dtype), [VMEM], VMEM, [], TICK_COST, "tick")(value)


def own_kernel(n_left, n_right, band, place, keep, *refs):
    earlies, refs = refs[:n_left], refs[n_left:]
    chunks = [refs[c * n_left : (c + 1) * n_left] for c in range(CHUNKS)]
    refs = refs[CHUNKS * n_left :]
    rights, refs = refs[:n_right], refs[n_right:]
    squares, sums, picks, panel, place_s, keep_s, product_a, product_b, sem, right_sem = refs
    me = lax.axis_index("row")
    depth = rights[0].shape[0]
    copies = [
        pltpu.make_async_copy(place, place_s, sem.at[0]),
        pltpu.make_async_copy(keep, keep_s, sem.at[1]),
    ]
    for k, right in enumerate(rights):
        at = pl.ds(pl.multiple_of((me ^ k) * depth, depth), depth)
        copies.append(pltpu.make_async_copy(right, panel.at[at, :], right_sem.at[k]))
    for copy in copies:
        copy.start()
    for copy in copies[2:]:
        copy.wait()
    bands = band // BS
    rows = squares.shape[0]
    partial = [jnp.zeros((8, BS), jnp.float32) for _ in range(COLB)]
    for q in range(rows // band):
        product = (product_a, product_b)[q % 2]
        chunk, first = divmod(q * band * CHUNKS, rows)
        deep = jnp.concatenate(
            [left[pl.ds(q * band, band), :] for left in earlies]
            + [left[pl.ds(first // CHUNKS, band), :] for left in chunks[chunk]],
            axis=1,
        )
        product[...] = product_of(deep, panel)
        if q == 0:
            for copy in copies[:2]:
                copy.wait()
        for i in range(bands):
            for s in range(KOL):
                row = q * bands + i
                block = place_s[s, row]
                picks[pl.ds(row * KOL + s, 1), :] = jnp.full((1, BS), block, jnp.int32)
                columns = pl.ds(pl.multiple_of(block * BS, BS), BS)
                picked = product[pl.ds(i * BS, BS), columns]
                square = picked * picked * keep_s[s, row].astype(jnp.float32)
                squares[pl.ds(row * BS, BS), pl.ds(s * BS, BS)] = square
                total = jnp.sum(square.reshape(BS // 8, 8, BS), axis=0)
                for c in range(COLB):
                    partial[c] = partial[c] + jnp.where(block == c, total, jnp.zeros_like(total))
    for c in range(COLB):
        sums[pl.ds(c, 1), :] = jnp.sum(partial[c], axis=0, keepdims=True)


def own_squares(place, keep, earlies, chunks, rights, band):
    rows = earlies[0].shape[0]
    inner = rights[0].shape[0] * len(rights)
    lefts = list(earlies) + [left for chunk in chunks for left in chunk]
    return call(
        functools.partial(own_kernel, len(earlies), len(rights), band),
        (
            jax.ShapeDtypeStruct((rows, OUT), jnp.float32),
            jax.ShapeDtypeStruct((COLB, BS), jnp.float32),
            jax.ShapeDtypeStruct((rows // BS * KOL, BS), jnp.int32),
        ),
        [HBM, HBM] + [VMEM] * len(lefts) + [HBM] + [pl.BlockSpec(memory_space=pl.ANY)] * (len(rights) - 1),
        (VMEM, VMEM, VMEM),
        [
            pltpu.VMEM((inner, TILE), jnp.bfloat16),
            pltpu.SMEM(place.shape, jnp.int32),
            pltpu.SMEM(place.shape, jnp.int32),
            pltpu.VMEM((band, TILE), jnp.float32),
            pltpu.VMEM((band, TILE), jnp.float32),
            pltpu.SemaphoreType.DMA((2,)),
            pltpu.SemaphoreType.DMA((len(rights),)),
        ],
        OWN_COST,
        "own",
    )(*in_hbm(place, keep), *lefts, *in_hbm(rights[0]), *rights[1:])


def row_scales(picks, sums, total_rows):
    scale = 1.0 / (sums / jnp.float32(total_rows) + 1e-6)
    rows = jnp.broadcast_to(scale[0:1, :], picks.shape)
    for c in range(1, COLB):
        rows = jnp.where(picks == c, scale[c : c + 1, :], rows)
    return rows


def scaled(squares, first, scales, target):
    for i in range(target.shape[0] // BS):
        for s in range(KOL):
            at = (pl.ds(first + i * BS, BS), pl.ds(s * BS, BS))
            to = (pl.ds(i * BS, BS), pl.ds(s * BS, BS))
            j = i * KOL + s
            target[to] = (squares[at] * scales[j : j + 1, :]).astype(target.dtype)


def scale_kernel(total_rows, sums, other, meta, squares, picks, sent, own, message):
    layer = lax.axis_index("layer")
    whole = sums[...] + other[...]
    message[0:COLB, :] = whole
    message[COLB : COLB + 2 * KOL, :] = meta[...]
    band = own.shape[0]
    jobs = band // BS * KOL
    for part, target in ((1, sent), (0, own)):
        mine = layer ^ part
        chosen = picks[pl.ds(pl.multiple_of(mine * jobs, jobs), jobs), :]
        scales = row_scales(chosen, whole, total_rows)
        scaled(squares, pl.multiple_of(mine * band, band), scales, target)


def scale_own(sums, other, meta, squares, picks, band, total_rows):
    return call(
        functools.partial(scale_kernel, total_rows),
        (
            jax.ShapeDtypeStruct((band, OUT), jnp.bfloat16),
            jax.ShapeDtypeStruct((band, OUT), jnp.bfloat16),
            jax.ShapeDtypeStruct((COLB + 2 * KOL, BS), jnp.float32),
        ),
        [VMEM] * 5,
        (VMEM, VMEM, VMEM),
        [],
        SCALE_COST,
        "scale",
    )(sums, other, meta, squares, picks)


def far_tile(message, scales, rights, deep, product, message_s, copy, total_rows, result, writes):
    layer = lax.axis_index("layer")
    me = lax.axis_index("row")
    scales[...] = 1.0 / (message[0:COLB, :] / jnp.float32(total_rows) + 1e-6)
    depth = rights[0].shape[0]
    bands = deep.shape[0] // BS
    whole = None
    for k, right in enumerate(rights):
        columns = pl.ds(pl.multiple_of((me ^ k) * depth, depth), depth)
        term = jnp.dot(deep[:, columns], right[...], preferred_element_type=jnp.float32)
        whole = term if whole is None else whole + term
    product[...] = whole
    copy.wait()
    for i in range(bands):
        rows = pl.ds(i * BS, BS)
        for s in range(KOL):
            row = layer * bands + i
            block = message_s[COLB + s, row].astype(jnp.int32)
            weight = scales[pl.ds(block, 1), :] * message_s[COLB + KOL + s, row]
            picked = product[rows, pl.ds(pl.multiple_of(block * BS, BS), BS)]
            result[rows, pl.ds(s * BS, BS)] = (picked * picked * weight).astype(result.dtype)
        writes[i].start()


def band_writes(result, out, bit, sem):
    writes = []
    for i in range(result.shape[0] // BS):
        rows = pl.ds(i * BS, BS)
        writes.append(pltpu.make_async_copy(result.at[rows, :], out.at[rows, tile_columns(bit)], sem.at[i]))
    return writes


def tile_columns(bit):
    return pl.ds(pl.multiple_of((lax.axis_index("layer") ^ bit) * OUT, OUT), OUT)


def far_kernel(n_left, n_right, total_rows, message, own, *refs):
    earlies, refs = refs[:n_left], refs[n_left:]
    chunks = [refs[c * n_left : (c + 1) * n_left] for c in range(CHUNKS)]
    refs = refs[CHUNKS * n_left :]
    rights, refs = refs[:n_right], refs[n_right:]
    out, deep, scales, product, result, message_s, message_sem, sem, write_sem = refs
    layer = lax.axis_index("layer")
    me = lax.axis_index("col")
    load = pltpu.make_async_copy(message, message_s, message_sem)
    load.start()
    own_copy = pltpu.make_async_copy(own, out.at[:, tile_columns(0)], sem)
    own_copy.start()
    band = deep.shape[0]
    own_rows = pl.ds(pl.multiple_of(layer * band, band), band)
    for k, left in enumerate(earlies):
        deep[:, pl.ds(pl.multiple_of((me ^ k) * BS, BS), BS)] = left[own_rows, :]
    per = chunks[0][0].shape[0] // band
    for c in range(CHUNKS):

        @pl.when(layer // per == c)
        def _():
            rows = pl.ds(pl.multiple_of((layer % per) * band, band), band)
            for k, left in enumerate(chunks[c]):
                deep[:, pl.ds(pl.multiple_of((me ^ (n_left + k)) * BS, BS), BS)] = left[rows, :]

    writes = band_writes(result, out, 2, write_sem)
    far_tile(message, scales, rights, deep, product, message_s, load, total_rows, result, writes)
    own_copy.wait()
    for write in writes:
        write.wait()


def far_tiles(message, own, earlies, chunks, rights, layers, total_rows):
    lefts = list(earlies) + [left for chunk in chunks for left in chunk]
    inner = 2 * len(earlies) * BS
    band = own.shape[0]
    return call(
        functools.partial(far_kernel, len(earlies), len(rights), total_rows),
        (
            jax.ShapeDtypeStruct((band, layers * OUT), jnp.bfloat16),
            jax.ShapeDtypeStruct((band, inner), jnp.bfloat16),
        ),
        [VMEM] * (2 + len(lefts) + len(rights)),
        (HBM, VMEM),
        [
            pltpu.VMEM((COLB, BS), jnp.float32),
            pltpu.VMEM((band, TILE), jnp.float32),
            pltpu.VMEM((band, OUT), jnp.bfloat16),
            pltpu.SMEM(message.shape, jnp.float32),
            pltpu.SemaphoreType.DMA,
            pltpu.SemaphoreType.DMA,
            pltpu.SemaphoreType.DMA((band // BS,)),
        ],
        FAR_COST,
        "far",
    )(message, own, *lefts, *rights)


def last_kernel(n_right, total_rows, message, sent, deep, *refs):
    rights, refs = refs[:n_right], refs[n_right:]
    _, out, scales, product, result, message_s, message_sem, sem, write_sem = refs
    load = pltpu.make_async_copy(message, message_s, message_sem)
    load.start()
    sent_copy = pltpu.make_async_copy(sent, out.at[:, tile_columns(1)], sem)
    sent_copy.start()
    writes = band_writes(result, out, 3, write_sem)
    far_tile(message, scales, rights, deep, product, message_s, load, total_rows, result, writes)
    sent_copy.wait()
    for write in writes:
        write.wait()


def last_tiles(message, sent, deep, rights, out, total_rows):
    band = deep.shape[0]
    return call(
        functools.partial(last_kernel, len(rights), total_rows),
        jax.ShapeDtypeStruct(out.shape, out.dtype),
        [VMEM] * (3 + len(rights)) + [HBM],
        HBM,
        [
            pltpu.VMEM((COLB, BS), jnp.float32),
            pltpu.VMEM((band, TILE), jnp.float32),
            pltpu.VMEM((band, OUT), jnp.bfloat16),
            pltpu.SMEM(message.shape, jnp.float32),
            pltpu.SemaphoreType.DMA,
            pltpu.SemaphoreType.DMA,
            pltpu.SemaphoreType.DMA((band // BS,)),
        ],
        FAR_COST,
        "last",
        {3 + len(rights): 0},
    )(message, sent, deep, *rights, out)


def shards(
    source_matrix_strip,
    target_matrix_strip,
    stored_tile_flag,
    target_place_tile_index,
    retained_target_flag,
):
    layers = lax.axis_size("layer")
    total_rows = source_matrix_strip.shape[0] * lax.axis_size("row")
    band = source_matrix_strip.shape[0] // layers
    place = target_place_tile_index.T
    keep = retained_target_flag.T
    half = lax.axis_size("col") // 2
    whole, masked, meta = mask_blocks(stored_tile_flag.T, source_matrix_strip, place, keep)
    target = target_matrix_strip
    across = [swap(piece, "col", half, "left_across") for piece in masked]
    far = swap(target, "layer", 2, "right_far")
    near = gather(target, "row", "right_near")
    earlies = spread(whole, "col", half, "left_early")
    far, across[0] = together(far, across[0])
    lates = [spread(piece, "col", half, "left_late") for piece in across]
    opposite = swap(far, "layer", 1, "right_opposite")
    far_pieces = gather(far, "row", "right_far_row")
    squares, sums, picks = own_squares(place, keep, earlies, lates, near, band)
    bit = lax.axis_size("row") // 2
    while bit > 1:
        sums = sums + swap(sums, "row", bit, "sums_row")
        bit //= 2
    other = swap(sums, "row", 1, "sums_row")
    far_pieces[-1], opposite, other = together(far_pieces[-1], opposite, other)
    sent, own, message = scale_own(sums, other, meta, squares, picks, band, total_rows)
    sent = swap(sent, "layer", 1, "sent")
    opposite_pieces = gather(opposite, "row", "right_opposite_row")
    messages = [swap(message, "layer", 2, "sums_far"), swap(message, "layer", 3, "sums_opposite")]
    out, deep = far_tiles(messages[0], own, earlies, lates, far_pieces, layers, total_rows)
    return last_tiles(messages[1], sent, deep, opposite_pieces, out, total_rows)


def solution(mesh):
    placed = (
        P("row", "col"),
        P("row", ("col", "layer")),
        P("row", "col"),
        P("row", ("col", "layer")),
        P("row", ("col", "layer")),
    )
    return jax.shard_map(
        shards, mesh=mesh, in_specs=placed, out_specs=P(("row", "layer"), "col"), check_vma=False
    )
```

```python
import functools

import jax
import jax.numpy as jnp
from jax import lax
from jax.experimental import pallas as pl
from jax.experimental.pallas import tpu as pltpu
from jax.sharding import PartitionSpec as P

BS = 128
CHUNKS = 2
COLB = 4
KOL = 2
TILE = COLB * BS
OUT = KOL * BS
MASK_COST, OWN_COST, SCALE_COST, FAR_COST, TICK_COST = 0, 0, 0, 0, 10**11
VMEM_LIMIT = 12 * 1024 * 1024

HBM = pl.BlockSpec(memory_space=pltpu.HBM)
VMEM = pl.BlockSpec(memory_space=pltpu.VMEM)


def swap(value, axis, bit, name):
    count = lax.axis_size(axis)
    with jax.named_scope(name):
        return lax.ppermute(value, axis, [(i, i ^ bit) for i in range(count)])


def spread(piece, axis, count, name):
    pieces = {0: piece}
    bit = count // 2
    while bit:
        for k in list(pieces):
            pieces[k ^ bit] = swap(pieces[k], axis, bit, name)
        bit //= 2
    return [pieces[k] for k in range(count)]


def gather(piece, axis, name):
    return spread(piece, axis, lax.axis_size(axis), name)


def together(*values):
    return lax.optimization_barrier(values)


def in_hbm(*values):
    return [pltpu.with_memory_space_constraint(value, pltpu.HBM) for value in values]


def call(kernel, out_shape, in_specs, out_specs, scratch, cost, name, aliases=None):
    return pl.pallas_call(
        kernel,
        out_shape=out_shape,
        in_specs=in_specs,
        out_specs=out_specs,
        scratch_shapes=scratch,
        input_output_aliases=aliases or {},
        compiler_params=pltpu.CompilerParams(vmem_limit_bytes=VMEM_LIMIT),
        cost_estimate=pl.CostEstimate(flops=cost, bytes_accessed=0, transcendentals=0),
        name=name,
    )


def mask_kernel(flag, source, target, place, keep, masked, *refs):
    chunks, refs = refs[:CHUNKS], refs[CHUNKS:]
    target_v, meta, flag_s, panel, meta_v, sem, flag_sem, meta_sem = refs
    parts = sem.shape[0]
    rows = source.shape[0] // parts
    flag_copy = pltpu.make_async_copy(flag, flag_s, flag_sem)
    flag_copy.start()
    copies = []
    for c in range(parts):
        part = pl.ds(c * rows, rows)
        copies.append(pltpu.make_async_copy(source.at[part, :], panel.at[part, :], sem.at[c]))
        copies[c].start()
    metas = [
        pltpu.make_async_copy(place, meta_v.at[0:KOL, :], meta_sem.at[0]),
        pltpu.make_async_copy(keep, meta_v.at[KOL : 2 * KOL, :], meta_sem.at[1]),
        pltpu.make_async_copy(target, target_v, meta_sem.at[2]),
    ]
    for copy in metas:
        copy.start()
    flag_copy.wait()
    for c in range(parts):
        copies[c].wait()
        for i in range(c * rows // BS, (c + 1) * rows // BS):
            at = pl.ds(i * BS, BS)
            block = panel[at, :]
            block = jnp.where(flag_s[0, i] != 0, block, jnp.zeros_like(block))
            masked[at, :] = block
            chunk, first = divmod(i * BS * CHUNKS, source.shape[0])
            chunks[chunk][pl.ds(first // CHUNKS, BS), :] = block
    for copy in metas:
        copy.wait()
    meta[...] = jnp.zeros_like(meta)
    meta[:, 0 : meta_v.shape[1]] = meta_v[...].astype(jnp.float32)


def mask_blocks(flag, source, target, place, keep):
    rows = source.shape[0]
    whole, *chunks, target_v, meta = call(
        mask_kernel,
        [jax.ShapeDtypeStruct(source.shape, source.dtype)]
        + [jax.ShapeDtypeStruct((rows // CHUNKS, BS), source.dtype)] * CHUNKS
        + [
            jax.ShapeDtypeStruct(target.shape, target.dtype),
            jax.ShapeDtypeStruct((2 * KOL, BS), jnp.float32),
        ],
        [HBM] * 5,
        [VMEM] * (CHUNKS + 3),
        [
            pltpu.SMEM(flag.shape, jnp.int32),
            pltpu.VMEM(source.shape, source.dtype),
            pltpu.VMEM((2 * KOL, place.shape[1]), jnp.int32),
            pltpu.SemaphoreType.DMA((4,)),
            pltpu.SemaphoreType.DMA,
            pltpu.SemaphoreType.DMA((3,)),
        ],
        MASK_COST,
        "mask",
    )(*in_hbm(flag, source, target, place, keep))
    return whole, chunks, target_v, meta


def right_blocks(rights, inner):
    me = lax.axis_index("col")
    depth = rights[0].shape[0]
    per = depth // BS
    blocks = []
    for group in range(inner // depth):
        piece = (me // per) ^ group ^ lax.axis_index("row")
        chosen = rights[0][...]
        for k in range(1, len(rights)):
            chosen = jnp.where(piece == k, rights[k][...], chosen)
        blocks.append(chosen)
    return blocks


def tick_kernel(before, after):
    after[...] = before[...]


def tick(value):
    return call(tick_kernel, jax.ShapeDtypeStruct(value.shape, value.dtype), [VMEM], VMEM, [], TICK_COST, "tick")(value)


def own_kernel(n_left, n_right, band, meta, *refs):
    earlies, refs = refs[:n_left], refs[n_left:]
    chunks = [refs[c * n_left : (c + 1) * n_left] for c in range(CHUNKS)]
    refs = refs[CHUNKS * n_left :]
    rights, refs = refs[:n_right], refs[n_right:]
    squares, sums, picks, panel, meta_s, product_a, product_b, sem = refs
    load = pltpu.make_async_copy(meta, meta_s, sem)
    load.start()
    inner = panel.shape[0]
    depth = rights[0].shape[0]
    me = lax.axis_index("col")
    for group, piece in enumerate(right_blocks(rights, inner)):
        panel[pl.ds(group * depth, depth), :] = piece
    per = depth // BS
    ordered = []
    for k in range(inner // BS):
        place = (k // per) * depth + ((me ^ k) % per) * BS
        ordered.append(panel[pl.ds(pl.multiple_of(place, BS), BS), :])
    right = jnp.concatenate(ordered, axis=0)
    bands = band // BS
    rows = squares.shape[0]
    partial = [jnp.zeros((8, BS), jnp.float32) for _ in range(COLB)]
    for q in range(rows // band):
        product = (product_a, product_b)[q % 2]
        chunk, first = divmod(q * band * CHUNKS, rows)
        deep = jnp.concatenate(
            [left[pl.ds(q * band, band), :] for left in earlies]
            + [left[pl.ds(first // CHUNKS, band), :] for left in chunks[chunk]],
            axis=1,
        )
        product[...] = jnp.dot(deep, right, preferred_element_type=jnp.float32)
        if q == 0:
            load.wait()
        for i in range(bands):
            for s in range(KOL):
                row = q * bands + i
                block = meta_s[s, row].astype(jnp.int32)
                picks[pl.ds(row * KOL + s, 1), :] = jnp.full((1, BS), block, jnp.int32)
                columns = pl.ds(pl.multiple_of(block * BS, BS), BS)
                picked = product[pl.ds(i * BS, BS), columns]
                square = picked * picked * meta_s[KOL + s, row]
                squares[pl.ds(row * BS, BS), pl.ds(s * BS, BS)] = square
                total = jnp.sum(square.reshape(BS // 8, 8, BS), axis=0)
                for c in range(COLB):
                    partial[c] = partial[c] + jnp.where(block == c, total, jnp.zeros_like(total))
    for c in range(COLB):
        sums[pl.ds(c, 1), :] = jnp.sum(partial[c], axis=0, keepdims=True)


def own_squares(meta, earlies, chunks, rights, band):
    rows = earlies[0].shape[0]
    inner = rights[0].shape[0] * len(rights)
    lefts = list(earlies) + [left for chunk in chunks for left in chunk]
    return call(
        functools.partial(own_kernel, len(earlies), len(rights), band),
        (
            jax.ShapeDtypeStruct((rows, OUT), jnp.float32),
            jax.ShapeDtypeStruct((COLB, BS), jnp.float32),
            jax.ShapeDtypeStruct((rows // BS * KOL, BS), jnp.int32),
        ),
        [VMEM] * (1 + len(lefts) + len(rights)),
        (VMEM, VMEM, VMEM),
        [
            pltpu.VMEM((inner, TILE), jnp.bfloat16),
            pltpu.SMEM(meta.shape, jnp.float32),
            pltpu.VMEM((band, TILE), jnp.float32),
            pltpu.VMEM((band, TILE), jnp.float32),
            pltpu.SemaphoreType.DMA,
        ],
        OWN_COST,
        "own",
    )(meta, *lefts, *rights)


def row_scales(picks, sums, total_rows):
    scale = 1.0 / (sums / jnp.float32(total_rows) + 1e-6)
    rows = jnp.broadcast_to(scale[0:1, :], picks.shape)
    for c in range(1, COLB):
        rows = jnp.where(picks == c, scale[c : c + 1, :], rows)
    return rows


def scaled(squares, first, scales, target):
    for i in range(target.shape[0] // BS):
        for s in range(KOL):
            at = (pl.ds(first + i * BS, BS), pl.ds(s * BS, BS))
            to = (pl.ds(i * BS, BS), pl.ds(s * BS, BS))
            j = i * KOL + s
            target[to] = (squares[at] * scales[j : j + 1, :]).astype(target.dtype)


def scale_kernel(total_rows, sums, other, meta, squares, picks, sent, own, message):
    layer = lax.axis_index("layer")
    whole = sums[...] + other[...]
    message[0:COLB, :] = whole
    message[COLB : COLB + 2 * KOL, :] = meta[...]
    band = own.shape[0]
    jobs = band // BS * KOL
    for part, target in ((1, sent), (0, own)):
        mine = layer ^ part
        chosen = picks[pl.ds(pl.multiple_of(mine * jobs, jobs), jobs), :]
        scales = row_scales(chosen, whole, total_rows)
        scaled(squares, pl.multiple_of(mine * band, band), scales, target)


def scale_own(sums, other, meta, squares, picks, band, total_rows):
    return call(
        functools.partial(scale_kernel, total_rows),
        (
            jax.ShapeDtypeStruct((band, OUT), jnp.bfloat16),
            jax.ShapeDtypeStruct((band, OUT), jnp.bfloat16),
            jax.ShapeDtypeStruct((COLB + 2 * KOL, BS), jnp.float32),
        ),
        [VMEM] * 5,
        (VMEM, VMEM, VMEM),
        [],
        SCALE_COST,
        "scale",
    )(sums, other, meta, squares, picks)


def far_tile(message, scales, rights, deep, product, message_s, copy, total_rows, result, writes):
    layer = lax.axis_index("layer")
    me = lax.axis_index("row")
    scales[...] = 1.0 / (message[0:COLB, :] / jnp.float32(total_rows) + 1e-6)
    depth = rights[0].shape[0]
    bands = deep.shape[0] // BS
    whole = None
    for k, right in enumerate(rights):
        columns = pl.ds(pl.multiple_of((me ^ k) * depth, depth), depth)
        term = jnp.dot(deep[:, columns], right[...], preferred_element_type=jnp.float32)
        whole = term if whole is None else whole + term
    product[...] = whole
    copy.wait()
    for i in range(bands):
        rows = pl.ds(i * BS, BS)
        for s in range(KOL):
            row = layer * bands + i
            block = message_s[COLB + s, row].astype(jnp.int32)
            weight = scales[pl.ds(block, 1), :] * message_s[COLB + KOL + s, row]
            picked = product[rows, pl.ds(pl.multiple_of(block * BS, BS), BS)]
            result[rows, pl.ds(s * BS, BS)] = (picked * picked * weight).astype(result.dtype)
        writes[i].start()


def band_writes(result, out, bit, sem):
    writes = []
    for i in range(result.shape[0] // BS):
        rows = pl.ds(i * BS, BS)
        writes.append(pltpu.make_async_copy(result.at[rows, :], out.at[rows, tile_columns(bit)], sem.at[i]))
    return writes


def tile_columns(bit):
    return pl.ds(pl.multiple_of((lax.axis_index("layer") ^ bit) * OUT, OUT), OUT)


def far_kernel(n_left, n_right, total_rows, message, own, *refs):
    earlies, refs = refs[:n_left], refs[n_left:]
    chunks = [refs[c * n_left : (c + 1) * n_left] for c in range(CHUNKS)]
    refs = refs[CHUNKS * n_left :]
    rights, refs = refs[:n_right], refs[n_right:]
    out, deep, scales, product, result, message_s, message_sem, sem, write_sem = refs
    layer = lax.axis_index("layer")
    me = lax.axis_index("col")
    load = pltpu.make_async_copy(message, message_s, message_sem)
    load.start()
    own_copy = pltpu.make_async_copy(own, out.at[:, tile_columns(0)], sem)
    own_copy.start()
    band = deep.shape[0]
    own_rows = pl.ds(pl.multiple_of(layer * band, band), band)
    for k, left in enumerate(earlies):
        deep[:, pl.ds(pl.multiple_of((me ^ k) * BS, BS), BS)] = left[own_rows, :]
    per = chunks[0][0].shape[0] // band
    for c in range(CHUNKS):

        @pl.when(layer // per == c)
        def _():
            rows = pl.ds(pl.multiple_of((layer % per) * band, band), band)
            for k, left in enumerate(chunks[c]):
                deep[:, pl.ds(pl.multiple_of((me ^ (n_left + k)) * BS, BS), BS)] = left[rows, :]

    writes = band_writes(result, out, 2, write_sem)
    far_tile(message, scales, rights, deep, product, message_s, load, total_rows, result, writes)
    own_copy.wait()
    for write in writes:
        write.wait()


def far_tiles(message, own, earlies, chunks, rights, layers, total_rows):
    lefts = list(earlies) + [left for chunk in chunks for left in chunk]
    inner = 2 * len(earlies) * BS
    band = own.shape[0]
    return call(
        functools.partial(far_kernel, len(earlies), len(rights), total_rows),
        (
            jax.ShapeDtypeStruct((band, layers * OUT), jnp.bfloat16),
            jax.ShapeDtypeStruct((band, inner), jnp.bfloat16),
        ),
        [VMEM] * (2 + len(lefts) + len(rights)),
        (HBM, VMEM),
        [
            pltpu.VMEM((COLB, BS), jnp.float32),
            pltpu.VMEM((band, TILE), jnp.float32),
            pltpu.VMEM((band, OUT), jnp.bfloat16),
            pltpu.SMEM(message.shape, jnp.float32),
            pltpu.SemaphoreType.DMA,
            pltpu.SemaphoreType.DMA,
            pltpu.SemaphoreType.DMA((band // BS,)),
        ],
        FAR_COST,
        "far",
    )(message, own, *lefts, *rights)


def last_kernel(n_right, total_rows, message, sent, deep, *refs):
    rights, refs = refs[:n_right], refs[n_right:]
    _, out, scales, product, result, message_s, message_sem, sem, write_sem = refs
    load = pltpu.make_async_copy(message, message_s, message_sem)
    load.start()
    sent_copy = pltpu.make_async_copy(sent, out.at[:, tile_columns(1)], sem)
    sent_copy.start()
    writes = band_writes(result, out, 3, write_sem)
    far_tile(message, scales, rights, deep, product, message_s, load, total_rows, result, writes)
    sent_copy.wait()
    for write in writes:
        write.wait()


def last_tiles(message, sent, deep, rights, out, total_rows):
    band = deep.shape[0]
    return call(
        functools.partial(last_kernel, len(rights), total_rows),
        jax.ShapeDtypeStruct(out.shape, out.dtype),
        [VMEM] * (3 + len(rights)) + [HBM],
        HBM,
        [
            pltpu.VMEM((COLB, BS), jnp.float32),
            pltpu.VMEM((band, TILE), jnp.float32),
            pltpu.VMEM((band, OUT), jnp.bfloat16),
            pltpu.SMEM(message.shape, jnp.float32),
            pltpu.SemaphoreType.DMA,
            pltpu.SemaphoreType.DMA,
            pltpu.SemaphoreType.DMA((band // BS,)),
        ],
        FAR_COST,
        "last",
        {3 + len(rights): 0},
    )(message, sent, deep, *rights, out)


def shards(
    source_matrix_strip,
    target_matrix_strip,
    stored_tile_flag,
    target_place_tile_index,
    retained_target_flag,
):
    layers = lax.axis_size("layer")
    total_rows = source_matrix_strip.shape[0] * lax.axis_size("row")
    band = source_matrix_strip.shape[0] // layers
    place = target_place_tile_index.T
    keep = retained_target_flag.T
    half = lax.axis_size("col") // 2
    whole, masked, near_own, meta = mask_blocks(
        stored_tile_flag.T, source_matrix_strip, target_matrix_strip, place, keep
    )
    target = target_matrix_strip
    across = [swap(piece, "col", half, "left_across") for piece in masked]
    far = swap(target, "layer", 2, "right_far")
    near = [near_own, *gather(target, "row", "right_near")[1:]]
    earlies = spread(whole, "col", half, "left_early")
    far, across[0] = together(far, across[0])
    lates = [spread(piece, "col", half, "left_late") for piece in across]
    opposite = swap(far, "layer", 1, "right_opposite")
    far_pieces = gather(far, "row", "right_far_row")
    squares, sums, picks = own_squares(meta, earlies, lates, near, band)
    bit = lax.axis_size("row") // 2
    while bit > 1:
        sums = sums + swap(sums, "row", bit, "sums_row")
        bit //= 2
    other = swap(sums, "row", 1, "sums_row")
    far_pieces[-1], opposite, other = together(far_pieces[-1], opposite, other)
    sent, own, message = scale_own(sums, other, meta, squares, picks, band, total_rows)
    sent = swap(sent, "layer", 1, "sent")
    opposite_pieces = gather(opposite, "row", "right_opposite_row")
    messages = [swap(message, "layer", 2, "sums_far"), swap(message, "layer", 3, "sums_opposite")]
    out, deep = far_tiles(messages[0], own, earlies, lates, far_pieces, layers, total_rows)
    return last_tiles(messages[1], sent, deep, opposite_pieces, out, total_rows)


def solution(mesh):
    placed = (
        P("row", "col"),
        P("row", ("col", "layer")),
        P("row", "col"),
        P("row", ("col", "layer")),
        P("row", ("col", "layer")),
    )
    return jax.shard_map(
        shards, mesh=mesh, in_specs=placed, out_specs=P(("row", "layer"), "col"), check_vma=False
    )
```
